512 devices in a mesh: dp: 8 (over x, core), ctx: 64 (over y, z).
Axes of the slice: x: 4, y: 8, z: 8, core: 2. Of those that a mesh axis runs over, the one named last changes fastest.
Arguments:
- queries: bfloat16 [16, 4096, 2048], P('dp', 'ctx'), may hold values from -52 to 52
- key_rows: bfloat16 [16, 4096, 2048], P('dp', 'ctx'), may hold values from -4 to 4
- value_rows: bfloat16 [16, 4096, 2048], P('dp', 'ctx'), may hold values from -6 to 6
- out_grad: bfloat16 [16, 4096, 2048], P('dp', 'ctx'), may hold values from -64 to 64
- level_slope: float32 [16], replicated, may hold values from -0.5 to 0.5
Outputs:
- query_grad: bfloat16 [16, 4096, 2048], P('dp', 'ctx')
- key_grad: bfloat16 [16, 4096, 2048], P('dp', 'ctx')
- value_grad: bfloat16 [16, 4096, 2048], P('dp', 'ctx')
- slope_grad: float32 [16], replicated
The draws below stay inside these ranges and needn't reach their ends.
All inputs are finite; a program needn't handle non-finite values.
Results may differ from the reference program's by a relative error of at most 0.0075.
Values may be sent and summed in bfloat16 or wider, within the bound.
A program may use at most 64 MiB of HBM per device.

```python
import math
import jax
import jax.numpy as jnp
from jax import lax

HEADS = 16
BLOCK = 64
HD = 2048
SEQ = 4096
BATCH = 16
N_CTX = 64


def base_keys(key):
    base = jax.random.normal(jax.random.fold_in(key, 11), (BATCH, SEQ, HD), jnp.float32)
    return jnp.clip(base, -4.0, 4.0)


def draw_key_rows(key, part):
    base = base_keys(key)
    return base.astype(jnp.bfloat16)


def draw_queries(key, part):
    drawn = 2.5 * jnp.clip(jax.random.normal(jax.random.fold_in(key, 12), (BATCH, SEQ, HD), jnp.float32), -6.0, 6.0)
    return drawn.astype(jnp.bfloat16)


def draw_out_grad(key, part):
    rows = jnp.arange(BATCH, dtype=jnp.float32)
    ramp = jnp.exp(math.log(3.0) * rows / max(BATCH - 1, 1))
    base = jnp.clip(jax.random.normal(jax.random.fold_in(key, 13), (BATCH, SEQ, HD), jnp.float32), -4.0, 4.0)
    return (4.0 * ramp[:, None, None] * base).astype(jnp.bfloat16)


def block_scale(own_key, dims, shards, least, top_value):
    factor_of, own = 1.0, jax.random.fold_in(own_key, 6)
    for position, shards_of in shards:
        draws = jnp.exp(jax.random.uniform(jax.random.fold_in(own, position), (shards_of,), jnp.float32, least / len(shards), top_value / len(shards)))
        factor_of = factor_of * jnp.repeat(draws, dims[position] // shards_of).reshape([-1 if axis == position else 1 for axis in range(len(dims))])
    return factor_of


def bell_draw(stream_key, extent, scale, reach, split=(), kind=jnp.bfloat16):
    values = scale * jax.random.normal(stream_key, extent, jnp.float32)
    if split:
        values = values * block_scale(stream_key, extent, split, -0.22, 0.18)
    return jnp.clip(values, -reach, reach).astype(kind)


def setup_inputs(seed: int = 0) -> dict:
    streams_of = jax.random.split(jax.random.key(seed), 6)
    queries = draw_queries(jax.random.fold_in(streams_of[5], 71), 0)
    key_rows = draw_key_rows(jax.random.fold_in(streams_of[5], 71), 0)
    value_rows = bell_draw(streams_of[2], (BATCH, SEQ, HD), 1.0, 6.0, ((0, 8), (1, 64)))
    out_grad = draw_out_grad(jax.random.fold_in(streams_of[5], 71), 0)
    level_slope = jnp.clip(jax.random.uniform(streams_of[4], (HEADS,), jnp.float32, -0.5, 0.5), -0.5, 0.5)
    return dict(queries=queries, key_rows=key_rows, value_rows=value_rows, out_grad=out_grad, level_slope=level_slope)


def pair_mean(cells):
    shaped = cells.reshape(cells.shape[:-2] + (cells.shape[-2] // 2, 2, cells.shape[-1])).astype(jnp.float32)
    return ((shaped[..., 0, :] + shaped[..., 1, :]) * 0.5).astype(jnp.bfloat16)

def product(form, left, right):
    return jnp.einsum(form, left.astype(jnp.float32), right.astype(jnp.float32), precision=lax.Precision.HIGHEST)

def attend(query_set, key_set, value_set, grad_set, level_slope):
    seqs, block, width = query_set.shape
    heads = level_slope.shape[0]
    head = width // heads
    key_count = key_set.shape[1]
    scale = 1.0 / math.sqrt(head)
    query_four = query_set.reshape(seqs, block, heads, head)
    key_four = key_set.reshape(seqs, key_count, heads, head)
    value_four = value_set.reshape(seqs, key_count, heads, head)
    grad_four = grad_set.reshape(seqs, block, heads, head)
    column = jnp.arange(key_count, dtype=jnp.int32)
    level_of = column // block - 1
    sibling = jnp.maximum(level_of, 0)
    multiple = jnp.where(level_of < 0, 1.0, jnp.exp2(sibling.astype(jnp.float32)))
    bias = level_slope[:, None] * sibling.astype(jnp.float32)[None, :]
    raw = product('sqhd,skhd->shqk', query_four, key_four)
    scores = raw * scale + bias[None, :, None, :]
    top = lax.optimization_barrier(jnp.max(scores, axis=-1, keepdims=True))
    weights = multiple[None, None, None, :] * jnp.exp(scores - top)
    probs = weights / lax.optimization_barrier(jnp.sum(weights, axis=-1, keepdims=True))
    probs_low = probs.astype(jnp.bfloat16)
    output = product('shqk,skhd->sqhd', probs_low, value_four)
    delta = jnp.transpose(lax.optimization_barrier(jnp.sum(grad_four.astype(jnp.float32) * output, axis=-1)), (0, 2, 1))
    upstream = product('sqhd,skhd->shqk', grad_four, value_four)
    dscore = probs * (upstream - delta[..., None])
    slope_part = lax.optimization_barrier(jnp.sum(dscore * sibling.astype(jnp.float32)[None, None, None, :], axis=(0, 2, 3)))
    dscore_low = dscore.astype(jnp.bfloat16)
    query_part = (product('shqk,skhd->sqhd', dscore_low, key_four) * scale).reshape(seqs, block, width)
    key_part = (product('shqk,sqhd->skhd', dscore_low, query_four) * scale).reshape(seqs, key_count, width)
    value_part = product('shqk,sqhd->skhd', probs_low, grad_four).reshape(seqs, key_count, width)
    return (query_part, key_part, value_part, slope_part)

def partner_of(sent, level, blocks):
    shaped = sent.reshape(blocks // 2 ** (level + 1), 2, 2 ** level, BLOCK, HD)
    return shaped[:, ::-1].reshape(blocks, BLOCK, HD)

def chain(direct, levels, blocks):
    grad_now = jnp.zeros((blocks, BLOCK, HD), jnp.float32)
    for level in reversed(range(levels)):
        spread = jnp.broadcast_to(grad_now[:, :, None, :], (blocks, BLOCK, 2, HD)).reshape(blocks, 2 * BLOCK, HD) * 0.5
        lower = spread[:, :BLOCK]
        upper = spread[:, BLOCK:]
        flag = (jnp.arange(blocks, dtype=jnp.int32) // 2 ** level % 2 == 1)[:, None, None]
        own_half = jnp.where(flag, upper, lower)
        other_half = jnp.where(flag, lower, upper)
        sent = (other_half + direct[:, (level + 1) * BLOCK:(level + 2) * BLOCK]).astype(jnp.bfloat16)
        grad_now = own_half + partner_of(sent, level, blocks).astype(jnp.float32)
    return (grad_now + direct[:, :BLOCK]).astype(jnp.bfloat16).reshape(SEQ, HD)

def one_sequence(query_seq, key_seq, value_seq, grad_seq, level_slope):
    blocks = N_CTX
    levels = N_CTX.bit_length() - 1
    query_blocks = query_seq.reshape(blocks, BLOCK, HD)
    grad_blocks = grad_seq.reshape(blocks, BLOCK, HD)
    keys_by_level = [key_seq.reshape(blocks, BLOCK, HD)]
    values_by_level = [value_seq.reshape(blocks, BLOCK, HD)]
    for level in range(levels - 1):
        keys_by_level.append(pair_mean(keys_by_level[-1].reshape(blocks >> level + 1, 2 * BLOCK, HD)))
        values_by_level.append(pair_mean(values_by_level[-1].reshape(blocks >> level + 1, 2 * BLOCK, HD)))

    def per_block(index):
        key_list = [lax.dynamic_index_in_dim(keys_by_level[0], index, 0, keepdims=False)]
        value_list = [lax.dynamic_index_in_dim(values_by_level[0], index, 0, keepdims=False)]
        for level in range(levels):
            group = index // 2 ** level
            partner = (group + 1 - 2 * (group % 2)).astype(jnp.int32)
            key_list.append(lax.dynamic_index_in_dim(keys_by_level[level], partner, 0, keepdims=False))
            value_list.append(lax.dynamic_index_in_dim(values_by_level[level], partner, 0, keepdims=False))
        key_set = jnp.concatenate(key_list, axis=0)[None]
        value_set = jnp.concatenate(value_list, axis=0)[None]
        query_set = lax.dynamic_index_in_dim(query_blocks, index, 0, keepdims=False)[None]
        grad_set = lax.dynamic_index_in_dim(grad_blocks, index, 0, keepdims=False)[None]
        query_part, key_part, value_part, slope_part = attend(query_set, key_set, value_set, grad_set, level_slope)
        return (query_part[0], key_part[0], value_part[0], slope_part)
    query_all, key_all, value_all, slope_all = lax.map(per_block, jnp.arange(blocks, dtype=jnp.int32))
    query_grad = query_all.astype(jnp.bfloat16).reshape(SEQ, HD)
    key_grad = chain(key_all, levels, blocks)
    value_grad = chain(value_all, levels, blocks)
    return (query_grad, key_grad, value_grad, lax.optimization_barrier(jnp.sum(slope_all, axis=0)))

def reference(queries, key_rows, value_rows, out_grad, level_slope):

    def run(items):
        return one_sequence(items[0], items[1], items[2], items[3], level_slope)
    query_grad, key_grad, value_grad, slope_terms = lax.map(run, (queries, key_rows, value_rows, out_grad))
    return (query_grad, key_grad, value_grad, lax.optimization_barrier(jnp.sum(slope_terms, axis=0)))
```

```python
import functools
import math

import jax
import jax.numpy as jnp
from jax import lax
from jax.experimental import pallas as pl
from jax.experimental.pallas import tpu as pltpu
from jax.sharding import PartitionSpec as P

MESH = pl.DeviceIdType.MESH
F32 = jnp.float32
BF16 = jnp.bfloat16
N = 8
BLOCK = 64
WIDE = 256
HEAD = 128
PAIR = 2 * BLOCK
UPPER = 3 * BLOCK
KEYS = PAIR + 2 * BLOCK + UPPER
LOCAL = 4 * BLOCK + 2 * BLOCK
LOG2E = math.log2(math.e)


def ring(step):
    def one(index, carry):
        half = index // 2
        step(half + 1 + (index % 2) * (N - 2 - 2 * half))
        return carry

    lax.fori_loop(0, N - 1, one, 0)


def halving(rows, columns):
    row = lax.broadcasted_iota(jnp.int32, (rows, columns), 0)
    column = lax.broadcasted_iota(jnp.int32, (rows, columns), 1)
    return jnp.where(column // 2 == row, 0.5, 0.0).astype(BF16)


def dot(left, right, dims=((1,), (0,))):
    return lax.dot_general(left, right, (dims, ((), ())), preferred_element_type=F32)


def spread_local(rows):
    token = lax.broadcasted_iota(jnp.int32, (rows, LOCAL), 0)
    cell = lax.broadcasted_iota(jnp.int32, (rows, LOCAL), 1)
    first = cell < 4 * BLOCK
    have = jnp.where(first, token // 2, token // 4 + 4 * BLOCK)
    return jnp.where(have == cell, jnp.where(first, 0.5, 0.25), 0.0).astype(BF16)


def spread_upper(rows):
    token = lax.broadcasted_iota(jnp.int32, (rows, UPPER), 0)
    cell = lax.broadcasted_iota(jnp.int32, (rows, UPPER), 1)
    three = cell < BLOCK
    four = cell < 2 * BLOCK
    want = jnp.where(three, cell, jnp.where(four, cell % 32, cell % 16))
    have = jnp.where(three, token // 8, jnp.where(four, token // 16, token // 32))
    size = jnp.where(three, 0.125, jnp.where(four, 0.0625, 0.03125))
    return jnp.where(want == have, size, 0.0).astype(BF16)


def kernel(
    slope_ref, k_in, v_in, q_in, g_in,
    dq_out, dk_out, dv_out, slope_out,
    xb, l1, l2, y3, y4, y5, yb, spread1, spread2,
    token_acc, quad_acc, upper_acc, c_local, y_back, c_upper, ob,
    slope_acc, slope_z, slope_mid, slope_y, slope_top, slope_dp,
    own_sem, in_send, in_recv, y_send, y_recv, back_send, back_recv,
    out_own, out_send, out_recv, s_send, s_recv,
):
    dp = lax.axis_index("dp")
    ctx = lax.axis_index("ctx")
    z = ctx % N
    y = ctx // N
    ins = (k_in, v_in, q_in, g_in)
    outs = (dq_out, dk_out, dv_out)

    def at_z(d):
        return (z + d) % N

    def on_z(d):
        return (dp, y * N + at_z(d))

    def on_y(row):
        return (dp, row * N + z)

    def on_dp(d):
        return ((dp + d) % N, ctx)

    def columns(place):
        return pl.ds(pl.multiple_of(place * WIDE, WIDE), WIDE)

    def remote(src, dst, send, recv, device):
        return pltpu.make_async_remote_copy(
            src_ref=src, dst_ref=dst, send_sem=send, recv_sem=recv,
            device_id=device, device_id_type=MESH,
        )

    barrier = pltpu.get_barrier_semaphore()
    @ring
    def _(d):
        for device in (on_z(d), on_y((y + d) % N), on_dp(d)):
            pl.semaphore_signal(barrier, inc=1, device_id=device, device_id_type=MESH)

    pl.semaphore_wait(barrier, 3 * (N - 1))

    def own_copy(a):
        return pltpu.make_async_copy(ins[a].at[:, :, columns(z)], xb.at[a, :, z], own_sem.at[a])

    def in_copy(a, d):
        return remote(
            ins[a].at[:, :, columns(at_z(d))], xb.at[a, :, z],
            in_send.at[a, d], in_recv.at[a, d], on_z(d),
        )

    def in_arrival(a, d):
        return remote(
            ins[a].at[:, :, columns(at_z(d))], xb.at[a, :, (z + N - d) % N],
            in_send.at[a, d], in_recv.at[a, d], on_z(d),
        )

    for group in ((0, 1), (2, 3)):
        ring(lambda d, group=group: [in_copy(a, d).start() for a in group])
        for a in group:
            own_copy(a).start()

    spread1[...] = spread_local(N * BLOCK)
    spread2[...] = spread_upper(N * BLOCK)
    quad_acc[...] = jnp.zeros_like(quad_acc)
    upper_acc[...] = jnp.zeros_like(upper_acc)
    slope_acc[...] = jnp.zeros_like(slope_acc)

    for a in (0, 1):
        own_copy(a).wait()
        ring(lambda d, a=a: in_arrival(a, d).wait_recv())

    pool = halving(BLOCK, PAIR)
    pool4 = halving(32, 64)
    pool5 = halving(16, 32)

    def summarize(kv, s):
        for p in range(4):
            cells = xb[kv, s, 2 * p : 2 * p + 2].reshape(PAIR, WIDE)
            l1[kv, s, p] = dot(pool, cells).astype(BF16)
        for r in range(2):
            cells = l1[kv, s, 2 * r : 2 * r + 2].reshape(PAIR, WIDE)
            l2[kv, s, r] = dot(pool, cells).astype(BF16)
        third = dot(pool, l2[kv, s].reshape(PAIR, WIDE)).astype(BF16)
        fourth = dot(pool4, third).astype(BF16)
        y3[kv, s] = third
        y4[kv, s] = fourth
        y5[kv, s] = dot(pool5, fourth).astype(BF16)

    for kv in range(2):
        for s in range(2):
            summarize(kv, s)

    row3 = y + 1 - 2 * (y % 2)
    base4 = 2 * (y // 2 + 1 - 2 * ((y // 2) % 2))
    base5 = 4 * (1 - y // 4)

    def rows(start, size):
        return pl.ds(pl.multiple_of(start, size), size)

    def y_copies(recv_index_of_self):
        copies = [
            remote(y3, yb.at[:, :, pl.ds(0, 64)], y_send.at[0], y_recv.at[0], on_y(row3))
        ]
        for j in range(2):
            slot = y % 2 if recv_index_of_self else j
            copies.append(
                remote(
                    y4, yb.at[:, :, rows(64 + 32 * slot, 32)],
                    y_send.at[1 + j], y_recv.at[1 + slot], on_y(base4 + j),
                )
            )
        for j in range(4):
            slot = y % 4 if recv_index_of_self else j
            copies.append(
                remote(
                    y5, yb.at[:, :, rows(128 + 16 * slot, 16)],
                    y_send.at[3 + j], y_recv.at[3 + slot], on_y(base5 + j),
                )
            )
        return copies

    def back_copies(recv_index_of_self):
        copies = [
            remote(
                y_back.at[:, :, pl.ds(0, 64)], c_upper.at[:, :, pl.ds(0, 64)],
                back_send.at[0], back_recv.at[0], on_y(row3),
            )
        ]
        for j in range(2):
            slot = y % 2 if recv_index_of_self else j
            copies.append(
                remote(
                    y_back.at[:, :, pl.ds(64 + 32 * j, 32)],
                    c_upper.at[:, :, rows(64 + 32 * slot, 32)],
                    back_send.at[1 + j], back_recv.at[1 + slot], on_y(base4 + j),
                )
            )
        for j in range(4):
            slot = y % 4 if recv_index_of_self else j
            copies.append(
                remote(
                    y_back.at[:, :, pl.ds(128 + 16 * j, 16)],
                    c_upper.at[:, :, rows(128 + 16 * slot, 16)],
                    back_send.at[3 + j], back_recv.at[3 + slot], on_y(base5 + j),
                )
            )
        return copies

    for copy in y_copies(True):
        copy.start()
    for a in (2, 3):
        own_copy(a).wait()
        ring(lambda d, a=a: in_arrival(a, d).wait_recv())
    for copy in y_copies(False):
        copy.wait_recv()

    scale = 1.0 / math.sqrt(HEAD)
    groups = ((0, PAIR, 0),) + tuple(
        (PAIR + BLOCK * (level - 1), PAIR + BLOCK * level, level) for level in range(1, 6)
    )

    def attend(p, s):
        sibling = p + 1 - 2 * (p % 2)
        quad = 1 - p // 2
        sets = []
        for kv in range(2):
            sets.append(
                jnp.concatenate(
                    [
                        xb[kv, s, pl.ds(2 * p, 2)].reshape(PAIR, WIDE),
                        l1[kv, s, sibling],
                        l2[kv, s, quad],
                        yb[kv, s],
                    ],
                    axis=0,
                )
            )
        query_rows = xb[2, s, pl.ds(2 * p, 2)].reshape(PAIR, WIDE)
        grad_rows = xb[3, s, pl.ds(2 * p, 2)].reshape(PAIR, WIDE)
        for h in range(2):
            lanes = slice(h * HEAD, (h + 1) * HEAD)
            slope = slope_ref[2 * z + h]
            keys, values = sets[0][:, lanes], sets[1][:, lanes]
            query, grad = query_rows[:, lanes], grad_rows[:, lanes]
            raw = dot(keys, query, ((1,), (1,)))
            up = dot(values, grad, ((1,), (1,)))
            scores = []
            top = None
            for first, last, level in groups:
                part = raw[first:last] * (scale * LOG2E)
                if level:
                    part = part + (slope * (LOG2E * level) + float(level))
                scores.append(part)
                best = jnp.max(part, axis=0, keepdims=True)
                top = best if top is None else jnp.maximum(top, best)
            weights = [jnp.exp2(part - top) for part in scores]
            total = sum(jnp.sum(part, axis=0, keepdims=True) for part in weights)
            inverse = 1.0 / total
            probs = [part * inverse for part in weights]
            probs_low = [part.astype(BF16) for part in probs]
            ups = [up[first:last] for first, last, _ in groups]
            delta = sum(
                jnp.sum(low.astype(F32) * part, axis=0, keepdims=True)
                for low, part in zip(probs_low, ups)
            )
            ds = [prob * (part - delta) for prob, part in zip(probs, ups)]
            tilted = sum(
                float(level) * jnp.sum(part.reshape(BLOCK // 8, 8, HEAD), axis=0)
                for part, (_, _, level) in zip(ds, groups)
                if level
            )
            slope_acc[h] += tilted
            ds_low = jnp.concatenate([part.astype(BF16) for part in ds], axis=0)
            p_low = jnp.concatenate(probs_low, axis=0)
            query_part = dot(ds_low, keys, ((0,), (0,))) * scale
            ob[0, s, pl.ds(2 * p, 2), :, lanes] = query_part.astype(BF16).reshape(2, BLOCK, HEAD)
            for kv, part in ((0, dot(ds_low, query)), (1, dot(p_low, grad))):
                token_acc[kv, s, p, :, lanes] = part[:PAIR]
                c_local[kv, s, pl.ds(sibling * BLOCK, BLOCK), lanes] = part[
                    PAIR : PAIR + BLOCK
                ].astype(BF16)
                quad_acc[kv, s, quad, :, lanes] += part[PAIR + BLOCK : PAIR + 2 * BLOCK]
                upper_acc[kv, s, :, lanes] += part[PAIR + 2 * BLOCK :]

    for p in range(4):
        for s in range(2):
            attend(p, s)

    def out_copy(o, d):
        return remote(
            ob.at[o, :, at_z(d)], outs[o].at[:, :, columns(z)],
            out_send.at[o, d], out_recv.at[o, d], on_z(d),
        )

    def out_arrival(o, d):
        return remote(
            ob.at[o, :, at_z(d)], outs[o].at[:, :, columns((z + N - d) % N)],
            out_send.at[o, d], out_recv.at[o, d], on_z(d),
        )

    def out_copy_own(o):
        return pltpu.make_async_copy(ob.at[o, :, z], outs[o].at[:, :, columns(z)], out_own.at[o])

    def slope_copy(phase, src, dst, place, d, device):
        return remote(src, dst.at[place], s_send.at[phase, d], s_recv.at[phase, d], device)

    ring(lambda d: slope_copy(0, slope_acc, slope_z, z, d, on_z(d)).start())

    y_back[...] = upper_acc[...].astype(BF16)
    for copy in back_copies(True):
        copy.start()
    ring(lambda d: out_copy(0, d).start())
    out_copy_own(0).start()
    for kv in range(2):
        for s in range(2):
            for r in range(2):
                c_local[kv, s, 256 + 64 * r : 320 + 64 * r] = quad_acc[kv, s, r].astype(BF16)

    slope_z[z] = slope_acc[...]
    ring(lambda d: slope_copy(0, slope_acc, slope_z, (z + N - d) % N, d, on_z(d)).wait_recv())
    slope_mid[...] = jnp.sum(slope_z[...], axis=2).reshape(2 * N, HEAD)
    ring(lambda d: slope_copy(1, slope_mid, slope_y, y, d, on_y((y + d) % N)).start())

    for copy in back_copies(False):
        copy.wait_recv()
    for kv in (0, 1):
        for s in range(2):
            total = token_acc[kv, s].reshape(N * BLOCK, WIDE)
            total = total + dot(spread1[...], c_local[kv, s]) + dot(spread2[...], c_upper[kv, s])
            if kv == 0:
                total = total * scale
            ob[1 + kv, s] = total.astype(BF16).reshape(N, BLOCK, WIDE)
        ring(lambda d, kv=kv: out_copy(1 + kv, d).start())
        out_copy_own(1 + kv).start()

    slope_y[y] = slope_mid[...]
    ring(lambda d: slope_copy(1, slope_mid, slope_y, (y + N - d) % N, d, on_y((y + d) % N)).wait_recv())
    slope_top[...] = sum(slope_y[i] for i in range(N))
    ring(lambda d: slope_copy(2, slope_top, slope_dp, dp, d, on_dp(d)).start())
    slope_dp[dp] = slope_top[...]
    ring(lambda d: slope_copy(2, slope_top, slope_dp, (dp + N - d) % N, d, on_dp(d)).wait_recv())
    everything = sum(slope_dp[i] for i in range(N))
    slope_out[...] = jnp.broadcast_to(
        jnp.sum(everything, axis=1, keepdims=True), (2 * N, HEAD)
    )

    for o in range(3):
        out_copy_own(o).wait()
        ring(lambda d, o=o: out_arrival(o, d).wait_recv())
    for a in range(4):
        ring(lambda d, a=a: in_copy(a, d).wait_send())
    for copy in y_copies(True) + back_copies(True):
        copy.wait_send()
    for o in range(3):
        ring(lambda d, o=o: out_copy(o, d).wait_send())

    @ring
    def _(d):
        slope_copy(0, slope_acc, slope_z, z, d, on_z(d)).wait_send()
        slope_copy(1, slope_mid, slope_y, y, d, on_y((y + d) % N)).wait_send()
        slope_copy(2, slope_top, slope_dp, dp, d, on_dp(d)).wait_send()


def shards(queries, key_rows, value_rows, out_grad, level_slope):
    seqs = queries.shape[0]
    whole = jax.ShapeDtypeStruct(queries.shape, BF16)
    any_spec = pl.BlockSpec(memory_space=pl.ANY)
    dma = pltpu.SemaphoreType.DMA
    vmem = pltpu.VMEM
    query_grad, key_grad, value_grad, slopes = pl.pallas_call(
        kernel,
        out_shape=(whole, whole, whole, jax.ShapeDtypeStruct((2 * N, HEAD), F32)),
        in_specs=[pl.BlockSpec(memory_space=pltpu.SMEM)] + [any_spec] * 4,
        out_specs=(any_spec, any_spec, any_spec, pl.BlockSpec(memory_space=pltpu.VMEM)),
        scratch_shapes=[
            vmem((4, seqs, N, BLOCK, WIDE), BF16),
            vmem((2, seqs, 4, BLOCK, WIDE), BF16),
            vmem((2, seqs, 2, BLOCK, WIDE), BF16),
            vmem((2, seqs, 64, WIDE), BF16),
            vmem((2, seqs, 32, WIDE), BF16),
            vmem((2, seqs, 16, WIDE), BF16),
            vmem((2, seqs, UPPER, WIDE), BF16),
            vmem((N * BLOCK, LOCAL), BF16),
            vmem((N * BLOCK, UPPER), BF16),
            vmem((2, seqs, 4, PAIR, WIDE), F32),
            vmem((2, seqs, 2, BLOCK, WIDE), F32),
            vmem((2, seqs, UPPER, WIDE), F32),
            vmem((2, seqs, LOCAL, WIDE), BF16),
            vmem((2, seqs, UPPER, WIDE), BF16),
            vmem((2, seqs, UPPER, WIDE), BF16),
            vmem((3, seqs, N, BLOCK, WIDE), BF16),
            vmem((2, 8, HEAD), F32),
            vmem((N, 2, 8, HEAD), F32),
            vmem((2 * N, HEAD), F32),
            vmem((N, 2 * N, HEAD), F32),
            vmem((2 * N, HEAD), F32),
            vmem((N, 2 * N, HEAD), F32),
            dma((4,)),
            dma((4, N)),
            dma((4, N)),
            dma((7,)),
            dma((7,)),
            dma((7,)),
            dma((7,)),
            dma((3,)),
            dma((3, N)),
            dma((3, N)),
            dma((3, N)),
            dma((3, N)),
        ],
        compiler_params=pltpu.CompilerParams(
            collective_id=0, has_side_effects=True, vmem_limit_bytes=48 * 1024 * 1024
        ),
        name="hierarchical_attention",
    )(level_slope, key_rows, value_rows, queries, out_grad)
    return query_grad, key_grad, value_grad, slopes[:, 0]


def solution(mesh):
    placed = (P("dp", "ctx", None),) * 4 + (P(),)
    return jax.shard_map(
        shards,
        mesh=mesh,
        in_specs=placed,
        out_specs=(P("dp", "ctx", None),) * 3 + (P(),),
        check_vma=False,
    )
```

```python
import functools
import math

import jax
import jax.numpy as jnp
from jax import lax
from jax.experimental import pallas as pl
from jax.experimental.pallas import tpu as pltpu
from jax.sharding import PartitionSpec as P

MESH = pl.DeviceIdType.MESH
F32 = jnp.float32
BF16 = jnp.bfloat16
N = 8
BLOCK = 64
WIDE = 256
HEAD = 128
PAIR = 2 * BLOCK
UPPER = 3 * BLOCK
KEYS = PAIR + 2 * BLOCK + UPPER
LOCAL = 4 * BLOCK + 2 * BLOCK
LOG2E = math.log2(math.e)


def ring(step):
    def one(index, carry):
        step(index)
        return carry

    lax.fori_loop(1, N, one, 0)


def halving(rows, columns):
    row = lax.broadcasted_iota(jnp.int32, (rows, columns), 0)
    column = lax.broadcasted_iota(jnp.int32, (rows, columns), 1)
    return jnp.where(column // 2 == row, 0.5, 0.0).astype(BF16)


def dot(left, right, dims=((1,), (0,))):
    return lax.dot_general(left, right, (dims, ((), ())), preferred_element_type=F32)


def spread_local(rows):
    token = lax.broadcasted_iota(jnp.int32, (rows, LOCAL), 0)
    cell = lax.broadcasted_iota(jnp.int32, (rows, LOCAL), 1)
    first = cell < 4 * BLOCK
    have = jnp.where(first, token // 2, token // 4 + 4 * BLOCK)
    return jnp.where(have == cell, jnp.where(first, 0.5, 0.25), 0.0).astype(BF16)


def spread_upper(rows):
    token = lax.broadcasted_iota(jnp.int32, (rows, UPPER), 0)
    cell = lax.broadcasted_iota(jnp.int32, (rows, UPPER), 1)
    three = cell < BLOCK
    four = cell < 2 * BLOCK
    want = jnp.where(three, cell, jnp.where(four, cell % 32, cell % 16))
    have = jnp.where(three, token // 8, jnp.where(four, token // 16, token // 32))
    size = jnp.where(three, 0.125, jnp.where(four, 0.0625, 0.03125))
    return jnp.where(want == have, size, 0.0).astype(BF16)


def kernel(
    slope_ref, k_in, v_in, q_in, g_in,
    dq_out, dk_out, dv_out, slope_out,
    xb, l1, l2, y3, y4, y5, yb, spread1, spread2,
    token_acc, quad_acc, upper_acc, c_local, y_back, c_upper, ob,
    slope_acc, slope_y, slope_mid, slope_dp, slope_top, slope_z,
    own_sem, in_send, in_recv, y_send, y_recv, back_send, back_recv,
    out_own, out_send, out_recv, s_send, s_recv,
):
    dp = lax.axis_index("dp")
    ctx = lax.axis_index("ctx")
    z = ctx % N
    y = ctx // N
    ins = (k_in, v_in, q_in, g_in)
    outs = (dq_out, dk_out, dv_out)

    def at_z(e):
        place = z
        for bit in (1, 2, 4):
            place = place + (1 - 2 * ((z // bit) % 2)) * ((e // bit) % 2) * bit
        return place

    def on_z(e):
        return (dp, y * N + at_z(e))

    def on_y(row):
        return (dp, row * N + z)

    def on_dp(d):
        return ((dp + d) % N, ctx)

    def columns(place):
        return pl.ds(pl.multiple_of(place * WIDE, WIDE), WIDE)

    def remote(src, dst, send, recv, device):
        return pltpu.make_async_remote_copy(
            src_ref=src, dst_ref=dst, send_sem=send, recv_sem=recv,
            device_id=device, device_id_type=MESH,
        )

    barrier = pltpu.get_barrier_semaphore()
    @ring
    def _(d):
        for device in (on_z(d), on_y((y + d) % N), on_dp(d)):
            pl.semaphore_signal(barrier, inc=1, device_id=device, device_id_type=MESH)

    pl.semaphore_wait(barrier, 3 * (N - 1))

    def own_copy(a):
        return pltpu.make_async_copy(ins[a].at[:, :, columns(z)], xb.at[a, :, 0], own_sem.at[a])

    def in_copy(a, d):
        return remote(
            ins[a].at[:, :, columns(at_z(d))], xb.at[a, :, d],
            in_send.at[a, d], in_recv.at[a, d], on_z(d),
        )

    def arrive(a, p):
        if p == 0:
            own_copy(a).wait()
        else:
            in_copy(a, 2 * p).wait_recv()
        in_copy(a, 2 * p + 1).wait_recv()

    for group in ((0, 1), (2, 3)):
        ring(lambda d, group=group: [in_copy(a, d).start() for a in group])
        for a in group:
            own_copy(a).start()

    spread1[...] = spread_local(N * BLOCK)
    spread2[...] = spread_upper(N * BLOCK)
    quad_acc[...] = jnp.zeros_like(quad_acc)
    upper_acc[...] = jnp.zeros_like(upper_acc)
    slope_acc[...] = jnp.zeros_like(slope_acc)

    pool = halving(BLOCK, PAIR)
    pool4 = halving(32, 64)
    pool5 = halving(16, 32)

    for p in range(4):
        for kv in range(2):
            arrive(kv, p)
            for s in range(2):
                cells = xb[kv, s, 2 * p : 2 * p + 2].reshape(PAIR, WIDE)
                l1[kv, s, p] = dot(pool, cells).astype(BF16)
                if p % 2:
                    cells = l1[kv, s, p - 1 : p + 1].reshape(PAIR, WIDE)
                    l2[kv, s, p // 2] = dot(pool, cells).astype(BF16)
                if p == 3:
                    third = dot(pool, l2[kv, s].reshape(PAIR, WIDE)).astype(BF16)
                    fourth = dot(pool4, third).astype(BF16)
                    y3[kv, s] = third
                    y4[kv, s] = fourth
                    y5[kv, s] = dot(pool5, fourth).astype(BF16)

    row3 = y + 1 - 2 * (y % 2)
    base4 = 2 * (y // 2 + 1 - 2 * ((y // 2) % 2))
    base5 = 4 * (1 - y // 4)

    def rows(start, size):
        return pl.ds(pl.multiple_of(start, size), size)

    def y_copies(recv_index_of_self):
        copies = [
            remote(y3, yb.at[:, :, pl.ds(0, 64)], y_send.at[0], y_recv.at[0], on_y(row3))
        ]
        for j in range(2):
            slot = y % 2 if recv_index_of_self else j
            copies.append(
                remote(
                    y4, yb.at[:, :, rows(64 + 32 * slot, 32)],
                    y_send.at[1 + j], y_recv.at[1 + slot], on_y(base4 + j),
                )
            )
        for j in range(4):
            slot = y % 4 if recv_index_of_self else j
            copies.append(
                remote(
                    y5, yb.at[:, :, rows(128 + 16 * slot, 16)],
                    y_send.at[3 + j], y_recv.at[3 + slot], on_y(base5 + j),
                )
            )
        return copies

    def back_copies(recv_index_of_self):
        copies = [
            remote(
                y_back.at[:, :, pl.ds(0, 64)], c_upper.at[:, :, pl.ds(0, 64)],
                back_send.at[0], back_recv.at[0], on_y(row3),
            )
        ]
        for j in range(2):
            slot = y % 2 if recv_index_of_self else j
            copies.append(
                remote(
                    y_back.at[:, :, pl.ds(64 + 32 * j, 32)],
                    c_upper.at[:, :, rows(64 + 32 * slot, 32)],
                    back_send.at[1 + j], back_recv.at[1 + slot], on_y(base4 + j),
                )
            )
        for j in range(4):
            slot = y % 4 if recv_index_of_self else j
            copies.append(
                remote(
                    y_back.at[:, :, pl.ds(128 + 16 * j, 16)],
                    c_upper.at[:, :, rows(128 + 16 * slot, 16)],
                    back_send.at[3 + j], back_recv.at[3 + slot], on_y(base5 + j),
                )
            )
        return copies

    for copy in y_copies(True):
        copy.start()
    for copy in y_copies(False):
        copy.wait_recv()

    def out_copy(o, d):
        return remote(
            ob.at[o, :, d], outs[o].at[:, :, columns(z)],
            out_send.at[o, d], out_recv.at[o, d], on_z(d),
        )

    def out_arrival(o, d):
        return remote(
            ob.at[o, :, d], outs[o].at[:, :, columns(at_z(d))],
            out_send.at[o, d], out_recv.at[o, d], on_z(d),
        )

    def out_copy_own(o):
        return pltpu.make_async_copy(ob.at[o, :, 0], outs[o].at[:, :, columns(z)], out_own.at[o])

    scale = 1.0 / math.sqrt(HEAD)
    groups = ((0, PAIR, 0),) + tuple(
        (PAIR + BLOCK * (level - 1), PAIR + BLOCK * level, level) for level in range(1, 6)
    )

    def attend(p, s):
        sibling = p + 1 - 2 * (p % 2)
        quad = 1 - p // 2
        sets = []
        for kv in range(2):
            sets.append(
                jnp.concatenate(
                    [
                        xb[kv, s, pl.ds(2 * p, 2)].reshape(PAIR, WIDE),
                        l1[kv, s, sibling],
                        l2[kv, s, quad],
                        yb[kv, s],
                    ],
                    axis=0,
                )
            )
        query_rows = xb[2, s, pl.ds(2 * p, 2)].reshape(PAIR, WIDE)
        grad_rows = xb[3, s, pl.ds(2 * p, 2)].reshape(PAIR, WIDE)
        for h in range(2):
            lanes = slice(h * HEAD, (h + 1) * HEAD)
            slope = slope_ref[2 * z + h]
            keys, values = sets[0][:, lanes], sets[1][:, lanes]
            query, grad = query_rows[:, lanes], grad_rows[:, lanes]
            raw = dot(keys, query, ((1,), (1,)))
            up = dot(values, grad, ((1,), (1,)))
            scores = []
            top = None
            for first, last, level in groups:
                part = raw[first:last] * (scale * LOG2E)
                if level:
                    part = part + (slope * (LOG2E * level) + float(level))
                scores.append(part)
                best = jnp.max(part, axis=0, keepdims=True)
                top = best if top is None else jnp.maximum(top, best)
            weights = [jnp.exp2(part - top) for part in scores]
            total = sum(jnp.sum(part, axis=0, keepdims=True) for part in weights)
            inverse = 1.0 / total
            probs = [part * inverse for part in weights]
            probs_low = [part.astype(BF16) for part in probs]
            ups = [up[first:last] for first, last, _ in groups]
            delta = sum(
                jnp.sum(low.astype(F32) * part, axis=0, keepdims=True)
                for low, part in zip(probs_low, ups)
            )
            ds = [prob * (part - delta) for prob, part in zip(probs, ups)]
            tilted = sum(
                float(level) * jnp.sum(part.reshape(BLOCK // 8, 8, HEAD), axis=0)
                for part, (_, _, level) in zip(ds, groups)
                if level
            )
            slope_acc[h] += tilted
            ds_low = jnp.concatenate([part.astype(BF16) for part in ds], axis=0)
            p_low = jnp.concatenate(probs_low, axis=0)
            query_part = dot(ds_low, keys, ((0,), (0,))) * scale
            ob[0, s, pl.ds(2 * p, 2), :, lanes] = query_part.astype(BF16).reshape(2, BLOCK, HEAD)
            for kv, part in ((0, dot(ds_low, query)), (1, dot(p_low, grad))):
                token_acc[kv, s, p, :, lanes] = part[:PAIR]
                c_local[kv, s, pl.ds(sibling * BLOCK, BLOCK), lanes] = part[
                    PAIR : PAIR + BLOCK
                ].astype(BF16)
                quad_acc[kv, s, quad, :, lanes] += part[PAIR + BLOCK : PAIR + 2 * BLOCK]
                upper_acc[kv, s, :, lanes] += part[PAIR + 2 * BLOCK :]

    for p in range(4):
        for a in (2, 3):
            arrive(a, p)
        for s in range(2):
            attend(p, s)
        if p == 0:
            out_copy_own(0).start()
        else:
            out_copy(0, 2 * p).start()
        out_copy(0, 2 * p + 1).start()

    def slope_copy(phase, src, dst, place, d, device):
        return remote(src, dst.at[place], s_send.at[phase, d], s_recv.at[phase, d], device)

    def slope_y_copy(d, place):
        return slope_copy(0, slope_acc, slope_y, place, d, on_y((y + d) % N))

    def slope_dp_copy(d, place):
        return slope_copy(1, slope_mid, slope_dp, place, d, on_dp(d))

    def slope_z_copy(d, place):
        return slope_copy(2, slope_top, slope_z, place, d, on_z(d))

    y_back[...] = upper_acc[...].astype(BF16)
    for copy in back_copies(True):
        copy.start()
    ring(lambda d: slope_y_copy(d, y).start())
    slope_y[y] = slope_acc[...]
    for kv in range(2):
        for s in range(2):
            for r in range(2):
                c_local[kv, s, 256 + 64 * r : 320 + 64 * r] = quad_acc[kv, s, r].astype(BF16)
    for copy in back_copies(False):
        copy.wait_recv()
    for kv in (0, 1):
        for s in range(2):
            total = token_acc[kv, s].reshape(N * BLOCK, WIDE)
            total = total + dot(spread1[...], c_local[kv, s]) + dot(spread2[...], c_upper[kv, s])
            if kv == 0:
                total = total * scale
            ob[1 + kv, s] = total.astype(BF16).reshape(N, BLOCK, WIDE)
        if kv == 1:
            ring(lambda d: slope_dp_copy(d, (dp + N - d) % N).wait_recv())
            slope_top[...] = sum(slope_dp[i] for i in range(N))
            ring(lambda d: slope_z_copy(d, z).start())
            slope_z[z] = slope_top[...]
        ring(lambda d, kv=kv: out_copy(1 + kv, d).start())
        out_copy_own(1 + kv).start()
        if kv == 0:
            ring(lambda d: slope_y_copy(d, (y + N - d) % N).wait_recv())
            slope_mid[...] = sum(slope_y[i] for i in range(N))
            ring(lambda d: slope_dp_copy(d, dp).start())
            slope_dp[dp] = slope_mid[...]
    ring(lambda d: slope_z_copy(d, at_z(d)).wait_recv())
    for owner in range(N):
        for h in range(2):
            slope_out[2 * owner + h] = jnp.sum(slope_z[owner, h])

    for o in range(3):
        out_copy_own(o).wait()
        ring(lambda d, o=o: out_arrival(o, d).wait_recv())
    for a in range(4):
        ring(lambda d, a=a: in_copy(a, d).wait_send())
    for copy in y_copies(True) + back_copies(True):
        copy.wait_send()
    for o in range(3):
        ring(lambda d, o=o: out_copy(o, d).wait_send())

    ring(lambda d: slope_y_copy(d, y).wait_send())
    ring(lambda d: slope_dp_copy(d, dp).wait_send())
    ring(lambda d: slope_z_copy(d, z).wait_send())


def shards(queries, key_rows, value_rows, out_grad, level_slope):
    seqs = queries.shape[0]
    whole = jax.ShapeDtypeStruct(queries.shape, BF16)
    any_spec = pl.BlockSpec(memory_space=pltpu.HBM)
    dma = pltpu.SemaphoreType.DMA
    vmem = pltpu.VMEM
    query_grad, key_grad, value_grad, slopes = pl.pallas_call(
        kernel,
        out_shape=(whole, whole, whole, jax.ShapeDtypeStruct((2 * N,), F32)),
        in_specs=[pl.BlockSpec(memory_space=pltpu.SMEM)] + [any_spec] * 4,
        out_specs=(any_spec, any_spec, any_spec, pl.BlockSpec(memory_space=pltpu.SMEM)),
        scratch_shapes=[
            vmem((4, seqs, N, BLOCK, WIDE), BF16),
            vmem((2, seqs, 4, BLOCK, WIDE), BF16),
            vmem((2, seqs, 2, BLOCK, WIDE), BF16),
            vmem((2, seqs, 64, WIDE), BF16),
            vmem((2, seqs, 32, WIDE), BF16),
            vmem((2, seqs, 16, WIDE), BF16),
            vmem((2, seqs, UPPER, WIDE), BF16),
            vmem((N * BLOCK, LOCAL), BF16),
            vmem((N * BLOCK, UPPER), BF16),
            vmem((2, seqs, 4, PAIR, WIDE), F32),
            vmem((2, seqs, 2, BLOCK, WIDE), F32),
            vmem((2, seqs, UPPER, WIDE), F32),
            vmem((2, seqs, LOCAL, WIDE), BF16),
            vmem((2, seqs, UPPER, WIDE), BF16),
            vmem((2, seqs, UPPER, WIDE), BF16),
            vmem((3, seqs, N, BLOCK, WIDE), BF16),
            vmem((2, 8, HEAD), F32),
            vmem((N, 2, 8, HEAD), F32),
            vmem((2, 8, HEAD), F32),
            vmem((N, 2, 8, HEAD), F32),
            vmem((2, 8, HEAD), F32),
            vmem((N, 2, 8, HEAD), F32),
            dma((4,)),
            dma((4, N)),
            dma((4, N)),
            dma((7,)),
            dma((7,)),
            dma((7,)),
            dma((7,)),
            dma((3,)),
            dma((3, N)),
            dma((3, N)),
            dma((3, N)),
            dma((3, N)),
        ],
        compiler_params=pltpu.CompilerParams(
            collective_id=0, has_side_effects=True, vmem_limit_bytes=67043328
        ),
        name="hierarchical_attention",
    )(level_slope, key_rows, value_rows, queries, out_grad)
    return query_grad, key_grad, value_grad, slopes


def solution(mesh):
    placed = (P("dp", "ctx", None),) * 4 + (P(),)
    return jax.shard_map(
        shards,
        mesh=mesh,
        in_specs=placed,
        out_specs=(P("dp", "ctx", None),) * 3 + (P(),),
        check_vma=False,
    )
```

```python
import functools
import math

import jax
import jax.numpy as jnp
from jax import lax
from jax.experimental import pallas as pl
from jax.experimental.pallas import tpu as pltpu
from jax.sharding import PartitionSpec as P

MESH = pl.DeviceIdType.MESH
F32 = jnp.float32
BF16 = jnp.bfloat16
N = 8
BLOCK = 64
WIDE = 256
HEAD = 128
PAIR = 2 * BLOCK
UPPER = 3 * BLOCK
KEYS = PAIR + 2 * BLOCK + UPPER
LOCAL = 4 * BLOCK + 2 * BLOCK
LOG2E = math.log2(math.e)


def ring(step):
    def one(index, carry):
        step(index)
        return carry

    lax.fori_loop(1, N, one, 0)


def halving(rows, columns):
    row = lax.broadcasted_iota(jnp.int32, (rows, columns), 0)
    column = lax.broadcasted_iota(jnp.int32, (rows, columns), 1)
    return jnp.where(column // 2 == row, 0.5, 0.0).astype(BF16)


def dot(left, right, dims=((1,), (0,))):
    return lax.dot_general(left, right, (dims, ((), ())), preferred_element_type=F32)


def spread_local(rows):
    token = lax.broadcasted_iota(jnp.int32, (rows, LOCAL), 0)
    cell = lax.broadcasted_iota(jnp.int32, (rows, LOCAL), 1)
    first = cell < 4 * BLOCK
    have = jnp.where(first, token // 2, token // 4 + 4 * BLOCK)
    return jnp.where(have == cell, jnp.where(first, 0.5, 0.25), 0.0).astype(BF16)


def spread_upper(rows):
    token = lax.broadcasted_iota(jnp.int32, (rows, UPPER), 0)
    cell = lax.broadcasted_iota(jnp.int32, (rows, UPPER), 1)
    three = cell < BLOCK
    four = cell < 2 * BLOCK
    want = jnp.where(three, cell, jnp.where(four, cell % 32, cell % 16))
    have = jnp.where(three, token // 8, jnp.where(four, token // 16, token // 32))
    size = jnp.where(three, 0.125, jnp.where(four, 0.0625, 0.03125))
    return jnp.where(want == have, size, 0.0).astype(BF16)


def kernel(
    slope_in, k_in, v_in, q_in, g_in,
    dq_out, dk_out, dv_out, slope_out,
    xb, l1, l2, y3, y4, y5, yb, spread1, spread2,
    token_acc, quad_acc, upper_acc, c_local, y_back, c_upper, ob,
    slope_acc, slope_y, slope_mid, slope_dp, slope_top, slope_z,
    slope_ref, slope_sem, own_sem, in_send, in_recv, y_send, y_recv, back_send, back_recv,
    out_own, out_send, out_recv, s_send, s_recv,
):
    dp = lax.axis_index("dp")
    ctx = lax.axis_index("ctx")
    z = ctx % N
    y = ctx // N
    ins = (k_in, v_in, q_in, g_in)
    outs = (dq_out, dk_out, dv_out)

    def at_z(e):
        place = z
        for bit in (1, 2, 4):
            place = place + (1 - 2 * ((z // bit) % 2)) * ((e // bit) % 2) * bit
        return place

    def around(step):
        def one(index, carry):
            half = index // 2
            target = (z + half + 1 + (index % 2) * (N - 2 - 2 * half)) % N
            step(sum(((target // bit + z // bit) % 2) * bit for bit in (1, 2, 4)))
            return carry

        lax.fori_loop(0, N - 1, one, 0)

    def on_z(e):
        return (dp, y * N + at_z(e))

    def on_y(row):
        return (dp, row * N + z)

    def on_dp(d):
        return ((dp + d) % N, ctx)

    def columns(place):
        return pl.ds(pl.multiple_of(place * WIDE, WIDE), WIDE)

    def remote(src, dst, send, recv, device):
        return pltpu.make_async_remote_copy(
            src_ref=src, dst_ref=dst, send_sem=send, recv_sem=recv,
            device_id=device, device_id_type=MESH,
        )

    barrier = pltpu.get_barrier_semaphore()
    @ring
    def _(d):
        for device in (on_z(d), on_y((y + d) % N), on_dp(d)):
            pl.semaphore_signal(barrier, inc=1, device_id=device, device_id_type=MESH)

    pl.semaphore_wait(barrier, 3 * (N - 1))

    slope_copy_in = pltpu.make_async_copy(slope_in, slope_ref, slope_sem.at[0])
    slope_copy_in.start()

    def own_copy(a):
        return pltpu.make_async_copy(ins[a].at[:, :, columns(z)], xb.at[a, :, 0], own_sem.at[a])

    def in_copy(a, d):
        return remote(
            ins[a].at[:, :, columns(at_z(d))], xb.at[a, :, d],
            in_send.at[a, d], in_recv.at[a, d], on_z(d),
        )

    def arrive(a, p):
        if p == 0:
            own_copy(a).wait()
        else:
            in_copy(a, 2 * p).wait_recv()
        in_copy(a, 2 * p + 1).wait_recv()

    for group in ((0, 1), (2, 3)):
        around(lambda d, group=group: [in_copy(a, d).start() for a in group])
        for a in group:
            own_copy(a).start()

    spread1[...] = spread_local(N * BLOCK)
    spread2[...] = spread_upper(N * BLOCK)
    quad_acc[...] = jnp.zeros_like(quad_acc)
    upper_acc[...] = jnp.zeros_like(upper_acc)
    slope_acc[...] = jnp.zeros_like(slope_acc)

    pool = halving(BLOCK, PAIR)
    pool4 = halving(32, 64)
    pool5 = halving(16, 32)

    for p in range(4):
        for kv in range(2):
            arrive(kv, p)
            for s in range(2):
                cells = xb[kv, s, 2 * p : 2 * p + 2].reshape(PAIR, WIDE)
                l1[kv, s, p] = dot(pool, cells).astype(BF16)
                if p % 2:
                    cells = l1[kv, s, p - 1 : p + 1].reshape(PAIR, WIDE)
                    l2[kv, s, p // 2] = dot(pool, cells).astype(BF16)
                if p == 3:
                    third = dot(pool, l2[kv, s].reshape(PAIR, WIDE)).astype(BF16)
                    fourth = dot(pool4, third).astype(BF16)
                    y3[kv, s] = third
                    y4[kv, s] = fourth
                    y5[kv, s] = dot(pool5, fourth).astype(BF16)

    row3 = y + 1 - 2 * (y % 2)
    base4 = 2 * (y // 2 + 1 - 2 * ((y // 2) % 2))
    base5 = 4 * (1 - y // 4)

    def rows(start, size):
        return pl.ds(pl.multiple_of(start, size), size)

    def y_copies(recv_index_of_self):
        copies = [
            remote(y3, yb.at[:, :, pl.ds(0, 64)], y_send.at[0], y_recv.at[0], on_y(row3))
        ]
        for j in range(2):
            slot = y % 2 if recv_index_of_self else j
            copies.append(
                remote(
                    y4, yb.at[:, :, rows(64 + 32 * slot, 32)],
                    y_send.at[1 + j], y_recv.at[1 + slot], on_y(base4 + j),
                )
            )
        for j in range(4):
            slot = y % 4 if recv_index_of_self else j
            copies.append(
                remote(
                    y5, yb.at[:, :, rows(128 + 16 * slot, 16)],
                    y_send.at[3 + j], y_recv.at[3 + slot], on_y(base5 + j),
                )
            )
        return copies

    def back_copies(recv_index_of_self):
        copies = [
            remote(
                y_back.at[:, :, pl.ds(0, 64)], c_upper.at[:, :, pl.ds(0, 64)],
                back_send.at[0], back_recv.at[0], on_y(row3),
            )
        ]
        for j in range(2):
            slot = y % 2 if recv_index_of_self else j
            copies.append(
                remote(
                    y_back.at[:, :, pl.ds(64 + 32 * j, 32)],
                    c_upper.at[:, :, rows(64 + 32 * slot, 32)],
                    back_send.at[1 + j], back_recv.at[1 + slot], on_y(base4 + j),
                )
            )
        for j in range(4):
            slot = y % 4 if recv_index_of_self else j
            copies.append(
                remote(
                    y_back.at[:, :, pl.ds(128 + 16 * j, 16)],
                    c_upper.at[:, :, rows(128 + 16 * slot, 16)],
                    back_send.at[3 + j], back_recv.at[3 + slot], on_y(base5 + j),
                )
            )
        return copies

    for copy in y_copies(True):
        copy.start()
    slope_copy_in.wait()
    for copy in y_copies(False):
        copy.wait_recv()

    def out_copy(o, d):
        return remote(
            ob.at[o, :, d], outs[o].at[:, :, columns(z)],
            out_send.at[o, d], out_recv.at[o, d], on_z(d),
        )

    def out_arrival(o, d):
        return remote(
            ob.at[o, :, d], outs[o].at[:, :, columns(at_z(d))],
            out_send.at[o, d], out_recv.at[o, d], on_z(d),
        )

    def out_copy_own(o):
        return pltpu.make_async_copy(ob.at[o, :, 0], outs[o].at[:, :, columns(z)], out_own.at[o])

    scale = 1.0 / math.sqrt(HEAD)
    groups = ((0, PAIR, 0),) + tuple(
        (PAIR + BLOCK * (level - 1), PAIR + BLOCK * level, level) for level in range(1, 6)
    )

    def attend(p, s):
        sibling = p + 1 - 2 * (p % 2)
        quad = 1 - p // 2
        sets = []
        for kv in range(2):
            sets.append(
                jnp.concatenate(
                    [
                        xb[kv, s, pl.ds(2 * p, 2)].reshape(PAIR, WIDE),
                        l1[kv, s, sibling],
                        l2[kv, s, quad],
                        yb[kv, s],
                    ],
                    axis=0,
                )
            )
        query_rows = xb[2, s, pl.ds(2 * p, 2)].reshape(PAIR, WIDE)
        grad_rows = xb[3, s, pl.ds(2 * p, 2)].reshape(PAIR, WIDE)
        for h in range(2):
            lanes = slice(h * HEAD, (h + 1) * HEAD)
            slope = slope_ref[2 * z + h]
            keys, values = sets[0][:, lanes], sets[1][:, lanes]
            query, grad = query_rows[:, lanes], grad_rows[:, lanes]
            raw = dot(keys, query, ((1,), (1,)))
            up = dot(values, grad, ((1,), (1,)))
            scores = []
            top = None
            for first, last, level in groups:
                part = raw[first:last] * (scale * LOG2E)
                if level:
                    part = part + (slope * (LOG2E * level) + float(level))
                scores.append(part)
                best = jnp.max(part, axis=0, keepdims=True)
                top = best if top is None else jnp.maximum(top, best)
            weights = [jnp.exp2(part - top) for part in scores]
            total = sum(jnp.sum(part, axis=0, keepdims=True) for part in weights)
            inverse = 1.0 / total
            probs = [part * inverse for part in weights]
            probs_low = [part.astype(BF16) for part in probs]
            ups = [up[first:last] for first, last, _ in groups]
            delta = sum(
                jnp.sum(low.astype(F32) * part, axis=0, keepdims=True)
                for low, part in zip(probs_low, ups)
            )
            ds = [prob * (part - delta) for prob, part in zip(probs, ups)]
            tilted = sum(
                float(level) * jnp.sum(part.reshape(BLOCK // 8, 8, HEAD), axis=0)
                for part, (_, _, level) in zip(ds, groups)
                if level
            )
            slope_acc[h] += tilted
            ds_low = jnp.concatenate([part.astype(BF16) for part in ds], axis=0)
            p_low = jnp.concatenate(probs_low, axis=0)
            query_part = dot(ds_low, keys, ((0,), (0,))) * scale
            ob[0, s, pl.ds(2 * p, 2), :, lanes] = query_part.astype(BF16).reshape(2, BLOCK, HEAD)
            for kv, part in ((0, dot(ds_low, query)), (1, dot(p_low, grad))):
                token_acc[kv, s, p, :, lanes] = part[:PAIR]
                c_local[kv, s, pl.ds(sibling * BLOCK, BLOCK), lanes] = part[
                    PAIR : PAIR + BLOCK
                ].astype(BF16)
                quad_acc[kv, s, quad, :, lanes] += part[PAIR + BLOCK : PAIR + 2 * BLOCK]
                upper_acc[kv, s, :, lanes] += part[PAIR + 2 * BLOCK :]

    for p in range(4):
        for a in (2, 3):
            arrive(a, p)
        for s in range(2):
            attend(p, s)
        if p == 0:
            out_copy_own(0).start()
        else:
            out_copy(0, 2 * p).start()
        out_copy(0, 2 * p + 1).start()

    def slope_copy(phase, src, dst, place, d, device):
        return remote(src, dst.at[place], s_send.at[phase, d], s_recv.at[phase, d], device)

    def slope_y_copy(d, place):
        return slope_copy(0, slope_acc, slope_y, place, d, on_y((y + d) % N))

    def slope_dp_copy(d, place):
        return slope_copy(1, slope_mid, slope_dp, place, d, on_dp(d))

    def slope_z_copy(d, place):
        return slope_copy(2, slope_top, slope_z, place, d, on_z(d))

    y_back[...] = upper_acc[...].astype(BF16)
    for copy in back_copies(True):
        copy.start()
    ring(lambda d: slope_y_copy(d, y).start())
    slope_y[y] = slope_acc[...]
    for kv in range(2):
        for s in range(2):
            for r in range(2):
                c_local[kv, s, 256 + 64 * r : 320 + 64 * r] = quad_acc[kv, s, r].astype(BF16)
    for copy in back_copies(False):
        copy.wait_recv()
    for kv in (0, 1):
        for s in range(2):
            total = token_acc[kv, s].reshape(N * BLOCK, WIDE)
            total = total + dot(spread1[...], c_local[kv, s]) + dot(spread2[...], c_upper[kv, s])
            if kv == 0:
                total = total * scale
            ob[1 + kv, s] = total.astype(BF16).reshape(N, BLOCK, WIDE)
        if kv == 1:
            ring(lambda d: slope_dp_copy(d, (dp + N - d) % N).wait_recv())
            slope_top[...] = sum(slope_dp[i] for i in range(N))
            ring(lambda d: slope_z_copy(d, z).start())
            slope_z[z] = slope_top[...]
        around(lambda d, kv=kv: out_copy(1 + kv, d).start())
        out_copy_own(1 + kv).start()
        if kv == 0:
            ring(lambda d: slope_y_copy(d, (y + N - d) % N).wait_recv())
            slope_mid[...] = sum(slope_y[i] for i in range(N))
            ring(lambda d: slope_dp_copy(d, dp).start())
            slope_dp[dp] = slope_mid[...]
    ring(lambda d: slope_z_copy(d, at_z(d)).wait_recv())
    for owner in range(N):
        for h in range(2):
            slope_out[2 * owner + h] = jnp.sum(slope_z[owner, h])

    for o in range(3):
        out_copy_own(o).wait()
        ring(lambda d, o=o: out_arrival(o, d).wait_recv())
    for a in range(4):
        ring(lambda d, a=a: in_copy(a, d).wait_send())
    for copy in y_copies(True) + back_copies(True):
        copy.wait_send()
    for o in range(3):
        ring(lambda d, o=o: out_copy(o, d).wait_send())

    ring(lambda d: slope_y_copy(d, y).wait_send())
    ring(lambda d: slope_dp_copy(d, dp).wait_send())
    ring(lambda d: slope_z_copy(d, z).wait_send())


def hand_over(*refs):
    sem = refs[8]
    copies = [pltpu.make_async_copy(refs[i], refs[4 + i], sem.at[i]) for i in range(4)]
    for copy in copies:
        copy.start()
    for copy in copies:
        copy.wait()


def shards(queries, key_rows, value_rows, out_grad, level_slope):
    seqs = queries.shape[0]
    whole = jax.ShapeDtypeStruct(queries.shape, BF16)
    any_spec = pl.BlockSpec(memory_space=pltpu.HBM)
    dma = pltpu.SemaphoreType.DMA
    held = pltpu.with_memory_space_constraint
    vmem = pltpu.VMEM
    query_grad, key_grad, value_grad, slopes = pl.pallas_call(
        kernel,
        out_shape=(whole, whole, whole, jax.ShapeDtypeStruct((2 * N,), F32)),
        in_specs=[any_spec] * 5,
        out_specs=(any_spec, any_spec, any_spec, pl.BlockSpec(memory_space=pltpu.SMEM)),
        scratch_shapes=[
            vmem((4, seqs, N, BLOCK, WIDE), BF16),
            vmem((2, seqs, 4, BLOCK, WIDE), BF16),
            vmem((2, seqs, 2, BLOCK, WIDE), BF16),
            vmem((2, seqs, 64, WIDE), BF16),
            vmem((2, seqs, 32, WIDE), BF16),
            vmem((2, seqs, 16, WIDE), BF16),
            vmem((2, seqs, UPPER, WIDE), BF16),
            vmem((N * BLOCK, LOCAL), BF16),
            vmem((N * BLOCK, UPPER), BF16),
            vmem((2, seqs, 4, PAIR, WIDE), F32),
            vmem((2, seqs, 2, BLOCK, WIDE), F32),
            vmem((2, seqs, UPPER, WIDE), F32),
            vmem((2, seqs, LOCAL, WIDE), BF16),
            vmem((2, seqs, UPPER, WIDE), BF16),
            vmem((2, seqs, UPPER, WIDE), BF16),
            vmem((3, seqs, N, BLOCK, WIDE), BF16),
            vmem((2, 8, HEAD), F32),
            vmem((N, 2, 8, HEAD), F32),
            vmem((2, 8, HEAD), F32),
            vmem((N, 2, 8, HEAD), F32),
            vmem((2, 8, HEAD), F32),
            vmem((N, 2, 8, HEAD), F32),
            pltpu.SMEM((2 * N,), F32),
            dma((1,)),
            dma((4,)),
            dma((4, N)),
            dma((4, N)),
            dma((7,)),
            dma((7,)),
            dma((7,)),
            dma((7,)),
            dma((3,)),
            dma((3, N)),
            dma((3, N)),
            dma((3, N)),
            dma((3, N)),
        ],
        compiler_params=pltpu.CompilerParams(
            collective_id=0, has_side_effects=True, vmem_limit_bytes=48 * 1024 * 1024
        ),
        name="hierarchical_attention",
    )(*(held(a, pltpu.HBM) for a in (level_slope, key_rows, value_rows, queries, out_grad)))
    return pl.pallas_call(
        hand_over,
        out_shape=(whole, whole, whole, jax.ShapeDtypeStruct((2 * N,), F32)),
        in_specs=[pl.BlockSpec(memory_space=pl.ANY)] * 4,
        out_specs=(any_spec,) * 4,
        scratch_shapes=[dma((4,))],
        compiler_params=pltpu.CompilerParams(vmem_limit_bytes=1024 * 1024),
        name="hand_over",
    )(query_grad, key_grad, value_grad, slopes)


def solution(mesh):
    placed = (P("dp", "ctx", None),) * 4 + (P(),)
    return jax.shard_map(
        shards,
        mesh=mesh,
        in_specs=placed,
        out_specs=(P("dp", "ctx", None),) * 3 + (P(),),
        check_vma=False,
    )
```

```python
import functools
import math

import jax
import jax.numpy as jnp
from jax import lax
from jax.experimental import pallas as pl
from jax.experimental.pallas import tpu as pltpu
from jax.sharding import PartitionSpec as P

MESH = pl.DeviceIdType.MESH
F32 = jnp.float32
BF16 = jnp.bfloat16
N = 8
BLOCK = 64
WIDE = 256
HEAD = 128
PAIR = 2 * BLOCK
UPPER = 3 * BLOCK
KEYS = PAIR + 2 * BLOCK + UPPER
LOCAL = 4 * BLOCK + 2 * BLOCK
LOG2E = math.log2(math.e)
PAIRS = (0, 1, 3, 2)


def ring(step):
    def one(index, carry):
        step(index)
        return carry

    lax.fori_loop(1, N, one, 0)


def halving(rows, columns):
    row = lax.broadcasted_iota(jnp.int32, (rows, columns), 0)
    column = lax.broadcasted_iota(jnp.int32, (rows, columns), 1)
    return jnp.where(column // 2 == row, 0.5, 0.0).astype(BF16)


def dot(left, right, dims=((1,), (0,))):
    return lax.dot_general(left, right, (dims, ((), ())), preferred_element_type=F32)


def spread_local(rows):
    token = lax.broadcasted_iota(jnp.int32, (rows, LOCAL), 0)
    cell = lax.broadcasted_iota(jnp.int32, (rows, LOCAL), 1)
    first = cell < 4 * BLOCK
    have = jnp.where(first, token // 2, token // 4 + 4 * BLOCK)
    return jnp.where(have == cell, jnp.where(first, 0.5, 0.25), 0.0).astype(BF16)


def spread_upper(rows):
    token = lax.broadcasted_iota(jnp.int32, (rows, UPPER), 0)
    cell = lax.broadcasted_iota(jnp.int32, (rows, UPPER), 1)
    three = cell < BLOCK
    four = cell < 2 * BLOCK
    want = jnp.where(three, cell, jnp.where(four, cell % 32, cell % 16))
    have = jnp.where(three, token // 8, jnp.where(four, token // 16, token // 32))
    size = jnp.where(three, 0.125, jnp.where(four, 0.0625, 0.03125))
    return jnp.where(want == have, size, 0.0).astype(BF16)


def kernel(
    slope_in, k_in, v_in, q_in, g_in,
    dq_out, dk_out, dv_out, slope_out,
    xb, l1, l2, y3, y4, y5, yb, spread1, spread2,
    token_acc, quad_acc, upper_acc, c_local, y_back, c_upper, ob,
    slope_acc, slope_y, slope_mid, slope_dp, slope_top, slope_z,
    slope_ref, slope_sem, own_sem, in_send, in_recv, y_send, y_recv, back_send, back_recv,
    out_own, out_send, out_recv, s_send, s_recv,
):
    dp = lax.axis_index("dp")
    ctx = lax.axis_index("ctx")
    z = ctx % N
    y = ctx // N
    ins = (k_in, v_in, q_in, g_in)
    outs = (dq_out, dk_out, dv_out)

    def at_z(e):
        place = z
        for bit in (1, 2, 4):
            place = place + (1 - 2 * ((z // bit) % 2)) * ((e // bit) % 2) * bit
        return place

    def around(step):
        def one(index, carry):
            half = index // 2
            target = (z + half + 1 + (index % 2) * (N - 2 - 2 * half)) % N
            step(sum(((target // bit + z // bit) % 2) * bit for bit in (1, 2, 4)))
            return carry

        lax.fori_loop(0, N - 1, one, 0)

    def on_z(e):
        return (dp, y * N + at_z(e))

    def on_y(row):
        return (dp, row * N + z)

    def on_dp(d):
        return ((dp + d) % N, ctx)

    def columns(place):
        return pl.ds(pl.multiple_of(place * WIDE, WIDE), WIDE)

    def remote(src, dst, send, recv, device):
        return pltpu.make_async_remote_copy(
            src_ref=src, dst_ref=dst, send_sem=send, recv_sem=recv,
            device_id=device, device_id_type=MESH,
        )

    barrier = pltpu.get_barrier_semaphore()
    @ring
    def _(d):
        for device in (on_z(d), on_y((y + d) % N), on_dp(d)):
            pl.semaphore_signal(barrier, inc=1, device_id=device, device_id_type=MESH)

    pl.semaphore_wait(barrier, 3 * (N - 1))

    slope_copy_in = pltpu.make_async_copy(slope_in, slope_ref, slope_sem.at[0])
    slope_copy_in.start()

    def own_copy(a):
        return pltpu.make_async_copy(ins[a].at[:, :, columns(z)], xb.at[a, :, 0], own_sem.at[a])

    def in_copy(a, d):
        return remote(
            ins[a].at[:, :, columns(at_z(d))], xb.at[a, :, d],
            in_send.at[a, d], in_recv.at[a, d], on_z(d),
        )

    def arrive(a, p):
        if p == 0:
            own_copy(a).wait()
        else:
            in_copy(a, 2 * p).wait_recv()
        in_copy(a, 2 * p + 1).wait_recv()

    for group in ((0, 1), (2, 3)):
        around(lambda d, group=group: [in_copy(a, d).start() for a in group])
        for a in group:
            own_copy(a).start()

    spread1[...] = spread_local(N * BLOCK)
    spread2[...] = spread_upper(N * BLOCK)
    quad_acc[...] = jnp.zeros_like(quad_acc)
    upper_acc[...] = jnp.zeros_like(upper_acc)
    slope_acc[...] = jnp.zeros_like(slope_acc)

    pool = halving(BLOCK, PAIR)
    pool4 = halving(32, 64)
    pool5 = halving(16, 32)

    for p in PAIRS:
        for kv in range(2):
            arrive(kv, p)
            for s in range(2):
                cells = xb[kv, s, 2 * p : 2 * p + 2].reshape(PAIR, WIDE)
                l1[kv, s, p] = dot(pool, cells).astype(BF16)
                if p in (1, 2):
                    quad = p // 2
                    cells = l1[kv, s, 2 * quad : 2 * quad + 2].reshape(PAIR, WIDE)
                    l2[kv, s, quad] = dot(pool, cells).astype(BF16)
                if p == 2:
                    third = dot(pool, l2[kv, s].reshape(PAIR, WIDE)).astype(BF16)
                    fourth = dot(pool4, third).astype(BF16)
                    y3[kv, s] = third
                    y4[kv, s] = fourth
                    y5[kv, s] = dot(pool5, fourth).astype(BF16)

    row3 = y + 1 - 2 * (y % 2)
    base4 = 2 * (y // 2 + 1 - 2 * ((y // 2) % 2))
    base5 = 4 * (1 - y // 4)

    def rows(start, size):
        return pl.ds(pl.multiple_of(start, size), size)

    def y_copies(recv_index_of_self):
        copies = [
            remote(y3, yb.at[:, :, pl.ds(0, 64)], y_send.at[0], y_recv.at[0], on_y(row3))
        ]
        for j in range(2):
            slot = y % 2 if recv_index_of_self else j
            copies.append(
                remote(
                    y4, yb.at[:, :, rows(64 + 32 * slot, 32)],
                    y_send.at[1 + j], y_recv.at[1 + slot], on_y(base4 + j),
                )
            )
        for j in range(4):
            slot = y % 4 if recv_index_of_self else j
            copies.append(
                remote(
                    y5, yb.at[:, :, rows(128 + 16 * slot, 16)],
                    y_send.at[3 + j], y_recv.at[3 + slot], on_y(base5 + j),
                )
            )
        return copies

    def back_copies(recv_index_of_self):
        copies = [
            remote(
                y_back.at[:, :, pl.ds(0, 64)], c_upper.at[:, :, pl.ds(0, 64)],
                back_send.at[0], back_recv.at[0], on_y(row3),
            )
        ]
        for j in range(2):
            slot = y % 2 if recv_index_of_self else j
            copies.append(
                remote(
                    y_back.at[:, :, pl.ds(64 + 32 * j, 32)],
                    c_upper.at[:, :, rows(64 + 32 * slot, 32)],
                    back_send.at[1 + j], back_recv.at[1 + slot], on_y(base4 + j),
                )
            )
        for j in range(4):
            slot = y % 4 if recv_index_of_self else j
            copies.append(
                remote(
                    y_back.at[:, :, pl.ds(128 + 16 * j, 16)],
                    c_upper.at[:, :, rows(128 + 16 * slot, 16)],
                    back_send.at[3 + j], back_recv.at[3 + slot], on_y(base5 + j),
                )
            )
        return copies

    for copy in reversed(y_copies(True)):
        copy.start()
    slope_copy_in.wait()
    for copy in y_copies(False):
        copy.wait_recv()

    def out_copy(o, d):
        return remote(
            ob.at[o, :, d], outs[o].at[:, :, columns(z)],
            out_send.at[o, d], out_recv.at[o, d], on_z(d),
        )

    def out_arrival(o, d):
        return remote(
            ob.at[o, :, d], outs[o].at[:, :, columns(at_z(d))],
            out_send.at[o, d], out_recv.at[o, d], on_z(d),
        )

    def out_copy_own(o):
        return pltpu.make_async_copy(ob.at[o, :, 0], outs[o].at[:, :, columns(z)], out_own.at[o])

    scale = 1.0 / math.sqrt(HEAD)
    groups = ((0, PAIR, 0),) + tuple(
        (PAIR + BLOCK * (level - 1), PAIR + BLOCK * level, level) for level in range(1, 6)
    )

    def attend(p, s):
        sibling = p + 1 - 2 * (p % 2)
        quad = 1 - p // 2
        sets = []
        for kv in range(2):
            sets.append(
                jnp.concatenate(
                    [
                        xb[kv, s, pl.ds(2 * p, 2)].reshape(PAIR, WIDE),
                        l1[kv, s, sibling],
                        l2[kv, s, quad],
                        yb[kv, s],
                    ],
                    axis=0,
                )
            )
        query_rows = xb[2, s, pl.ds(2 * p, 2)].reshape(PAIR, WIDE)
        grad_rows = xb[3, s, pl.ds(2 * p, 2)].reshape(PAIR, WIDE)
        for h in range(2):
            lanes = slice(h * HEAD, (h + 1) * HEAD)
            slope = slope_ref[2 * z + h]
            keys, values = sets[0][:, lanes], sets[1][:, lanes]
            query, grad = query_rows[:, lanes], grad_rows[:, lanes]
            raw = dot(keys, query, ((1,), (1,)))
            up = dot(values, grad, ((1,), (1,)))
            scores = []
            top = None
            for first, last, level in groups:
                part = raw[first:last] * (scale * LOG2E)
                if level:
                    part = part + (slope * (LOG2E * level) + float(level))
                scores.append(part)
                best = jnp.max(part, axis=0, keepdims=True)
                top = best if top is None else jnp.maximum(top, best)
            weights = [jnp.exp2(part - top) for part in scores]
            total = sum(jnp.sum(part, axis=0, keepdims=True) for part in weights)
            inverse = 1.0 / total
            probs = [part * inverse for part in weights]
            probs_low = [part.astype(BF16) for part in probs]
            ups = [up[first:last] for first, last, _ in groups]
            delta = sum(
                jnp.sum(low.astype(F32) * part, axis=0, keepdims=True)
                for low, part in zip(probs_low, ups)
            )
            ds = [prob * (part - delta) for prob, part in zip(probs, ups)]
            tilted = sum(
                float(level) * jnp.sum(part.reshape(BLOCK // 8, 8, HEAD), axis=0)
                for part, (_, _, level) in zip(ds, groups)
                if level
            )
            slope_acc[h] += tilted
            ds_low = jnp.concatenate([part.astype(BF16) for part in ds], axis=0)
            p_low = jnp.concatenate(probs_low, axis=0)
            query_part = dot(ds_low, keys, ((0,), (0,))) * scale
            ob[0, s, pl.ds(2 * p, 2), :, lanes] = query_part.astype(BF16).reshape(2, BLOCK, HEAD)
            for kv, part in ((0, dot(ds_low, query)), (1, dot(p_low, grad))):
                token_acc[kv, s, p, :, lanes] = part[:PAIR]
                c_local[kv, s, pl.ds(sibling * BLOCK, BLOCK), lanes] = part[
                    PAIR : PAIR + BLOCK
                ].astype(BF16)
                quad_acc[kv, s, quad, :, lanes] += part[PAIR + BLOCK : PAIR + 2 * BLOCK]
                upper_acc[kv, s, :, lanes] += part[PAIR + 2 * BLOCK :]

    for p in PAIRS:
        for a in (2, 3):
            arrive(a, p)
        for s in range(2):
            attend(p, s)
        if p == 0:
            out_copy_own(0).start()
        else:
            out_copy(0, 2 * p).start()
        out_copy(0, 2 * p + 1).start()

    def slope_copy(phase, src, dst, place, d, device):
        return remote(src, dst.at[place], s_send.at[phase, d], s_recv.at[phase, d], device)

    def slope_y_copy(d, place):
        return slope_copy(0, slope_acc, slope_y, place, d, on_y((y + d) % N))

    def slope_dp_copy(d, place):
        return slope_copy(1, slope_mid, slope_dp, place, d, on_dp(d))

    def slope_z_copy(d, place):
        return slope_copy(2, slope_top, slope_z, place, d, on_z(d))

    y_back[...] = upper_acc[...].astype(BF16)
    for copy in reversed(back_copies(True)):
        copy.start()
    ring(lambda d: slope_y_copy(d, y).start())
    slope_y[y] = slope_acc[...]
    for kv in range(2):
        for s in range(2):
            for r in range(2):
                c_local[kv, s, 256 + 64 * r : 320 + 64 * r] = quad_acc[kv, s, r].astype(BF16)
    for kv in range(2):
        for s in range(2):
            below = dot(spread1[...], c_local[kv, s])
            token_acc[kv, s] += below.reshape(4, PAIR, WIDE)
    for copy in back_copies(False):
        copy.wait_recv()
    for kv in (0, 1):
        for s in range(2):
            total = token_acc[kv, s].reshape(N * BLOCK, WIDE)
            total = total + dot(spread2[...], c_upper[kv, s])
            if kv == 0:
                total = total * scale
            ob[1 + kv, s] = total.astype(BF16).reshape(N, BLOCK, WIDE)
        if kv == 1:
            ring(lambda d: slope_dp_copy(d, (dp + N - d) % N).wait_recv())
            slope_top[...] = sum(slope_dp[i] for i in range(N))
            ring(lambda d: slope_z_copy(d, z).start())
            slope_z[z] = slope_top[...]
        around(lambda d, kv=kv: out_copy(1 + kv, d).start())
        out_copy_own(1 + kv).start()
        if kv == 0:
            ring(lambda d: slope_y_copy(d, (y + N - d) % N).wait_recv())
            slope_mid[...] = sum(slope_y[i] for i in range(N))
            ring(lambda d: slope_dp_copy(d, dp).start())
            slope_dp[dp] = slope_mid[...]
    ring(lambda d: slope_z_copy(d, at_z(d)).wait_recv())
    for owner in range(N):
        for h in range(2):
            slope_out[2 * owner + h] = jnp.sum(slope_z[owner, h])

    for o in range(3):
        out_copy_own(o).wait()
        ring(lambda d, o=o: out_arrival(o, d).wait_recv())
    for a in range(4):
        ring(lambda d, a=a: in_copy(a, d).wait_send())
    for copy in y_copies(True) + back_copies(True):
        copy.wait_send()
    for o in range(3):
        ring(lambda d, o=o: out_copy(o, d).wait_send())

    ring(lambda d: slope_y_copy(d, y).wait_send())
    ring(lambda d: slope_dp_copy(d, dp).wait_send())
    ring(lambda d: slope_z_copy(d, z).wait_send())


def hand_over(*refs):
    sem = refs[8]
    copies = [pltpu.make_async_copy(refs[i], refs[4 + i], sem.at[i]) for i in range(4)]
    for copy in copies:
        copy.start()
    for copy in copies:
        copy.wait()


def shards(queries, key_rows, value_rows, out_grad, level_slope):
    seqs = queries.shape[0]
    whole = jax.ShapeDtypeStruct(queries.shape, BF16)
    any_spec = pl.BlockSpec(memory_space=pltpu.HBM)
    dma = pltpu.SemaphoreType.DMA
    held = pltpu.with_memory_space_constraint
    vmem = pltpu.VMEM
    query_grad, key_grad, value_grad, slopes = pl.pallas_call(
        kernel,
        out_shape=(whole, whole, whole, jax.ShapeDtypeStruct((2 * N,), F32)),
        in_specs=[any_spec] * 5,
        out_specs=(any_spec, any_spec, any_spec, pl.BlockSpec(memory_space=pltpu.SMEM)),
        scratch_shapes=[
            vmem((4, seqs, N, BLOCK, WIDE), BF16),
            vmem((2, seqs, 4, BLOCK, WIDE), BF16),
            vmem((2, seqs, 2, BLOCK, WIDE), BF16),
            vmem((2, seqs, 64, WIDE), BF16),
            vmem((2, seqs, 32, WIDE), BF16),
            vmem((2, seqs, 16, WIDE), BF16),
            vmem((2, seqs, UPPER, WIDE), BF16),
            vmem((N * BLOCK, LOCAL), BF16),
            vmem((N * BLOCK, UPPER), BF16),
            vmem((2, seqs, 4, PAIR, WIDE), F32),
            vmem((2, seqs, 2, BLOCK, WIDE), F32),
            vmem((2, seqs, UPPER, WIDE), F32),
            vmem((2, seqs, LOCAL, WIDE), BF16),
            vmem((2, seqs, UPPER, WIDE), BF16),
            vmem((2, seqs, UPPER, WIDE), BF16),
            vmem((3, seqs, N, BLOCK, WIDE), BF16),
            vmem((2, 8, HEAD), F32),
            vmem((N, 2, 8, HEAD), F32),
            vmem((2, 8, HEAD), F32),
            vmem((N, 2, 8, HEAD), F32),
            vmem((2, 8, HEAD), F32),
            vmem((N, 2, 8, HEAD), F32),
            pltpu.SMEM((2 * N,), F32),
            dma((1,)),
            dma((4,)),
            dma((4, N)),
            dma((4, N)),
            dma((7,)),
            dma((7,)),
            dma((7,)),
            dma((7,)),
            dma((3,)),
            dma((3, N)),
            dma((3, N)),
            dma((3, N)),
            dma((3, N)),
        ],
        compiler_params=pltpu.CompilerParams(
            collective_id=0, has_side_effects=True, vmem_limit_bytes=48 * 1024 * 1024
        ),
        name="hierarchical_attention",
    )(*(held(a, pltpu.HBM) for a in (level_slope, key_rows, value_rows, queries, out_grad)))
    return pl.pallas_call(
        hand_over,
        out_shape=(whole, whole, whole, jax.ShapeDtypeStruct((2 * N,), F32)),
        in_specs=[pl.BlockSpec(memory_space=pl.ANY)] * 4,
        out_specs=(any_spec,) * 4,
        scratch_shapes=[dma((4,))],
        compiler_params=pltpu.CompilerParams(vmem_limit_bytes=1024 * 1024),
        name="hand_over",
    )(query_grad, key_grad, value_grad, slopes)


def solution(mesh):
    placed = (P("dp", "ctx", None),) * 4 + (P(),)
    return jax.shard_map(
        shards,
        mesh=mesh,
        in_specs=placed,
        out_specs=(P("dp", "ctx", None),) * 3 + (P(),),
        check_vma=False,
    )
```

```python
import functools
import math

import jax
import jax.numpy as jnp
from jax import lax
from jax.experimental import pallas as pl
from jax.experimental.pallas import tpu as pltpu
from jax.sharding import PartitionSpec as P

MESH = pl.DeviceIdType.MESH
F32 = jnp.float32
BF16 = jnp.bfloat16
N = 8
BLOCK = 64
WIDE = 256
HEAD = 128
PAIR = 2 * BLOCK
UPPER = 3 * BLOCK
KEYS = PAIR + 2 * BLOCK + UPPER
LOCAL = 4 * BLOCK + 2 * BLOCK
LOG2E = math.log2(math.e)
PAIRS = (0, 1, 3, 2)


def ring(step):
    def one(index, carry):
        step(index)
        return carry

    lax.fori_loop(1, N, one, 0)


def halving(rows, columns):
    row = lax.broadcasted_iota(jnp.int32, (rows, columns), 0)
    column = lax.broadcasted_iota(jnp.int32, (rows, columns), 1)
    return jnp.where(column // 2 == row, 0.5, 0.0).astype(BF16)


def dot(left, right, dims=((1,), (0,))):
    return lax.dot_general(left, right, (dims, ((), ())), preferred_element_type=F32)


def spread_local(rows):
    token = lax.broadcasted_iota(jnp.int32, (rows, LOCAL), 0)
    cell = lax.broadcasted_iota(jnp.int32, (rows, LOCAL), 1)
    first = cell < 4 * BLOCK
    have = jnp.where(first, token // 2, token // 4 + 4 * BLOCK)
    return jnp.where(have == cell, jnp.where(first, 0.5, 0.25), 0.0).astype(BF16)


def spread_upper(rows):
    token = lax.broadcasted_iota(jnp.int32, (rows, UPPER), 0)
    cell = lax.broadcasted_iota(jnp.int32, (rows, UPPER), 1)
    three = cell < BLOCK
    four = cell < 2 * BLOCK
    want = jnp.where(three, cell, jnp.where(four, cell % 32, cell % 16))
    have = jnp.where(three, token // 8, jnp.where(four, token // 16, token // 32))
    size = jnp.where(three, 0.125, jnp.where(four, 0.0625, 0.03125))
    return jnp.where(want == have, size, 0.0).astype(BF16)


def kernel(
    slope_in, k_in, v_in, q_in, g_in,
    dq_out, dk_out, dv_out, slope_out,
    xb, l1, l2, y3, y4, y5, yb, spread1, spread2,
    token_acc, quad_acc, upper_acc, c_local, y_back, c_upper, ob,
    slope_acc, slope_y, slope_mid, slope_dp, slope_top, slope_z,
    slope_ref, slope_sem, own_sem, in_send, in_recv, y_send, y_recv, back_send, back_recv,
    out_own, out_send, out_recv, s_send, s_recv,
):
    dp = lax.axis_index("dp")
    ctx = lax.axis_index("ctx")
    z = ctx % N
    y = ctx // N
    ins = (k_in, v_in, q_in, g_in)
    outs = (dq_out, dk_out, dv_out)

    def at_z(e):
        place = z
        for bit in (1, 2, 4):
            place = place + (1 - 2 * ((z // bit) % 2)) * ((e // bit) % 2) * bit
        return place

    def around(step):
        def one(index, carry):
            half = index // 2
            target = (z + half + 1 + (index % 2) * (N - 2 - 2 * half)) % N
            step(sum(((target // bit + z // bit) % 2) * bit for bit in (1, 2, 4)))
            return carry

        lax.fori_loop(0, N - 1, one, 0)

    def inward(step):
        def one(index, carry):
            half = index // 2
            target = (z + half + 1 + (index % 2) * (N - 2 - 2 * half)) % N
            step(sum(((target // bit + z // bit) % 2) * bit for bit in (1, 2, 4)))
            return carry

        lax.fori_loop(0, N - 1, lambda i, c: one(N - 2 - i, c), 0)

    def on_z(e):
        return (dp, y * N + at_z(e))

    def on_y(row):
        return (dp, row * N + z)

    def on_dp(d):
        return ((dp + d) % N, ctx)

    def columns(place):
        return pl.ds(pl.multiple_of(place * WIDE, WIDE), WIDE)

    def remote(src, dst, send, recv, device):
        return pltpu.make_async_remote_copy(
            src_ref=src, dst_ref=dst, send_sem=send, recv_sem=recv,
            device_id=device, device_id_type=MESH,
        )

    barrier = pltpu.get_barrier_semaphore()
    @ring
    def _(d):
        for device in (on_z(d), on_y((y + d) % N), on_dp(d)):
            pl.semaphore_signal(barrier, inc=1, device_id=device, device_id_type=MESH)

    pl.semaphore_wait(barrier, 3 * (N - 1))

    slope_copy_in = pltpu.make_async_copy(slope_in, slope_ref, slope_sem.at[0])
    slope_copy_in.start()

    def own_copy(a):
        return pltpu.make_async_copy(ins[a].at[:, :, columns(z)], xb.at[a, :, 0], own_sem.at[a])

    def in_copy(a, d):
        return remote(
            ins[a].at[:, :, columns(at_z(d))], xb.at[a, :, d],
            in_send.at[a, d], in_recv.at[a, d], on_z(d),
        )

    def arrive(a, p):
        if p == 0:
            own_copy(a).wait()
        else:
            in_copy(a, 2 * p).wait_recv()
        in_copy(a, 2 * p + 1).wait_recv()

    for group in ((0, 1), (2, 3)):
        around(lambda d, group=group: [in_copy(a, d).start() for a in group])
        for a in group:
            own_copy(a).start()

    spread1[...] = spread_local(N * BLOCK)
    spread2[...] = spread_upper(N * BLOCK)
    quad_acc[...] = jnp.zeros_like(quad_acc)
    upper_acc[...] = jnp.zeros_like(upper_acc)
    slope_acc[...] = jnp.zeros_like(slope_acc)

    pool = halving(BLOCK, PAIR)
    pool4 = halving(32, 64)
    pool5 = halving(16, 32)

    for p in PAIRS:
        for kv in range(2):
            arrive(kv, p)
            for s in range(2):
                cells = xb[kv, s, 2 * p : 2 * p + 2].reshape(PAIR, WIDE)
                l1[kv, s, p] = dot(pool, cells).astype(BF16)
                if p in (1, 2):
                    quad = p // 2
                    cells = l1[kv, s, 2 * quad : 2 * quad + 2].reshape(PAIR, WIDE)
                    l2[kv, s, quad] = dot(pool, cells).astype(BF16)
                if p == 2:
                    third = dot(pool, l2[kv, s].reshape(PAIR, WIDE)).astype(BF16)
                    fourth = dot(pool4, third).astype(BF16)
                    y3[kv, s] = third
                    y4[kv, s] = fourth
                    y5[kv, s] = dot(pool5, fourth).astype(BF16)

    row3 = y + 1 - 2 * (y % 2)
    base4 = 2 * (y // 2 + 1 - 2 * ((y // 2) % 2))
    base5 = 4 * (1 - y // 4)

    def rows(start, size):
        return pl.ds(pl.multiple_of(start, size), size)

    def y_copies(recv_index_of_self):
        copies = [
            remote(y3, yb.at[:, :, pl.ds(0, 64)], y_send.at[0], y_recv.at[0], on_y(row3))
        ]
        for j in range(2):
            slot = y % 2 if recv_index_of_self else j
            copies.append(
                remote(
                    y4, yb.at[:, :, rows(64 + 32 * slot, 32)],
                    y_send.at[1 + j], y_recv.at[1 + slot], on_y(base4 + j),
                )
            )
        for j in range(4):
            slot = y % 4 if recv_index_of_self else j
            copies.append(
                remote(
                    y5, yb.at[:, :, rows(128 + 16 * slot, 16)],
                    y_send.at[3 + j], y_recv.at[3 + slot], on_y(base5 + j),
                )
            )
        return copies

    def back_copies(recv_index_of_self):
        copies = [
            remote(
                y_back.at[:, :, pl.ds(0, 64)], c_upper.at[:, :, pl.ds(0, 64)],
                back_send.at[0], back_recv.at[0], on_y(row3),
            )
        ]
        for j in range(2):
            slot = y % 2 if recv_index_of_self else j
            copies.append(
                remote(
                    y_back.at[:, :, pl.ds(64 + 32 * j, 32)],
                    c_upper.at[:, :, rows(64 + 32 * slot, 32)],
                    back_send.at[1 + j], back_recv.at[1 + slot], on_y(base4 + j),
                )
            )
        for j in range(4):
            slot = y % 4 if recv_index_of_self else j
            copies.append(
                remote(
                    y_back.at[:, :, pl.ds(128 + 16 * j, 16)],
                    c_upper.at[:, :, rows(128 + 16 * slot, 16)],
                    back_send.at[3 + j], back_recv.at[3 + slot], on_y(base5 + j),
                )
            )
        return copies

    for copy in reversed(y_copies(True)):
        copy.start()
    slope_copy_in.wait()
    for copy in y_copies(False):
        copy.wait_recv()

    def out_copy(o, d):
        return remote(
            ob.at[o, :, d], outs[o].at[:, :, columns(z)],
            out_send.at[o, d], out_recv.at[o, d], on_z(d),
        )

    def out_arrival(o, d):
        return remote(
            ob.at[o, :, d], outs[o].at[:, :, columns(at_z(d))],
            out_send.at[o, d], out_recv.at[o, d], on_z(d),
        )

    def out_copy_own(o):
        return pltpu.make_async_copy(ob.at[o, :, 0], outs[o].at[:, :, columns(z)], out_own.at[o])

    scale = 1.0 / math.sqrt(HEAD)
    groups = ((0, PAIR, 0),) + tuple(
        (PAIR + BLOCK * (level - 1), PAIR + BLOCK * level, level) for level in range(1, 6)
    )

    def attend(p, s):
        sibling = p + 1 - 2 * (p % 2)
        quad = 1 - p // 2
        sets = []
        for kv in range(2):
            sets.append(
                jnp.concatenate(
                    [
                        xb[kv, s, pl.ds(2 * p, 2)].reshape(PAIR, WIDE),
                        l1[kv, s, sibling],
                        l2[kv, s, quad],
                        yb[kv, s],
                    ],
                    axis=0,
                )
            )
        query_rows = xb[2, s, pl.ds(2 * p, 2)].reshape(PAIR, WIDE)
        grad_rows = xb[3, s, pl.ds(2 * p, 2)].reshape(PAIR, WIDE)
        for h in range(2):
            lanes = slice(h * HEAD, (h + 1) * HEAD)
            slope = slope_ref[2 * z + h]
            keys, values = sets[0][:, lanes], sets[1][:, lanes]
            query, grad = query_rows[:, lanes], grad_rows[:, lanes]
            raw = dot(keys, query, ((1,), (1,)))
            up = dot(values, grad, ((1,), (1,)))
            scores = []
            top = None
            for first, last, level in groups:
                part = raw[first:last] * (scale * LOG2E)
                if level:
                    part = part + (slope * (LOG2E * level) + float(level))
                scores.append(part)
                best = jnp.max(part, axis=0, keepdims=True)
                top = best if top is None else jnp.maximum(top, best)
            weights = [jnp.exp2(part - top) for part in scores]
            total = sum(jnp.sum(part, axis=0, keepdims=True) for part in weights)
            inverse = 1.0 / total
            probs = [part * inverse for part in weights]
            probs_low = [part.astype(BF16) for part in probs]
            ups = [up[first:last] for first, last, _ in groups]
            delta = sum(
                jnp.sum(low.astype(F32) * part, axis=0, keepdims=True)
                for low, part in zip(probs_low, ups)
            )
            ds = [prob * (part - delta) for prob, part in zip(probs, ups)]
            tilted = sum(
                float(level) * jnp.sum(part.reshape(BLOCK // 8, 8, HEAD), axis=0)
                for part, (_, _, level) in zip(ds, groups)
                if level
            )
            slope_acc[h] += tilted
            ds_low = jnp.concatenate([part.astype(BF16) for part in ds], axis=0)
            p_low = jnp.concatenate(probs_low, axis=0)
            query_part = dot(ds_low, keys, ((0,), (0,))) * scale
            ob[0, s, pl.ds(2 * p, 2), :, lanes] = query_part.astype(BF16).reshape(2, BLOCK, HEAD)
            for kv, part in ((0, dot(ds_low, query)), (1, dot(p_low, grad))):
                token_acc[kv, s, p, :, lanes] = part[:PAIR]
                c_local[kv, s, pl.ds(sibling * BLOCK, BLOCK), lanes] = part[
                    PAIR : PAIR + BLOCK
                ].astype(BF16)
                quad_acc[kv, s, quad, :, lanes] += part[PAIR + BLOCK : PAIR + 2 * BLOCK]
                upper_acc[kv, s, :, lanes] += part[PAIR + 2 * BLOCK :]

    for p in PAIRS:
        for a in (2, 3):
            arrive(a, p)
        for s in range(2):
            attend(p, s)
        if p == 0:
            out_copy_own(0).start()
        else:
            out_copy(0, 2 * p).start()
        out_copy(0, 2 * p + 1).start()

    def slope_copy(phase, src, dst, place, d, device):
        return remote(src, dst.at[place], s_send.at[phase, d], s_recv.at[phase, d], device)

    def slope_y_copy(d, place):
        return slope_copy(0, slope_acc, slope_y, place, d, on_y((y + d) % N))

    def slope_dp_copy(d, place):
        return slope_copy(1, slope_mid, slope_dp, place, d, on_dp(d))

    def slope_z_copy(d, place):
        return slope_copy(2, slope_top, slope_z, place, d, on_z(d))

    y_back[...] = upper_acc[...].astype(BF16)
    for copy in reversed(back_copies(True)):
        copy.start()
    ring(lambda d: slope_y_copy(d, y).start())
    slope_y[y] = slope_acc[...]
    for kv in range(2):
        for s in range(2):
            for r in range(2):
                c_local[kv, s, 256 + 64 * r : 320 + 64 * r] = quad_acc[kv, s, r].astype(BF16)
    for kv in range(2):
        for s in range(2):
            below = dot(spread1[...], c_local[kv, s])
            token_acc[kv, s] += below.reshape(4, PAIR, WIDE)
    for copy in back_copies(False):
        copy.wait_recv()
    for kv in (0, 1):
        for s in range(2):
            total = token_acc[kv, s].reshape(N * BLOCK, WIDE)
            total = total + dot(spread2[...], c_upper[kv, s])
            if kv == 0:
                total = total * scale
            ob[1 + kv, s] = total.astype(BF16).reshape(N, BLOCK, WIDE)
        if kv == 1:
            ring(lambda d: slope_dp_copy(d, (dp + N - d) % N).wait_recv())
            slope_top[...] = sum(slope_dp[i] for i in range(N))
            ring(lambda d: slope_z_copy(d, z).start())
            slope_z[z] = slope_top[...]
        inward(lambda d, kv=kv: out_copy(1 + kv, d).start())
        out_copy_own(1 + kv).start()
        if kv == 0:
            ring(lambda d: slope_y_copy(d, (y + N - d) % N).wait_recv())
            slope_mid[...] = sum(slope_y[i] for i in range(N))
            ring(lambda d: slope_dp_copy(d, dp).start())
            slope_dp[dp] = slope_mid[...]
    ring(lambda d: slope_z_copy(d, at_z(d)).wait_recv())
    for owner in range(N):
        for h in range(2):
            slope_out[2 * owner + h] = jnp.sum(slope_z[owner, h])

    for a in range(4):
        ring(lambda d, a=a: in_copy(a, d).wait_send())
    for copy in y_copies(True) + back_copies(True):
        copy.wait_send()
    ring(lambda d: slope_y_copy(d, y).wait_send())
    ring(lambda d: slope_dp_copy(d, dp).wait_send())
    ring(lambda d: slope_z_copy(d, z).wait_send())
    for o in range(3):
        out_copy_own(o).wait()
        ring(lambda d, o=o: out_copy(o, d).wait_send())
    for o in range(3):
        ring(lambda d, o=o: out_arrival(o, d).wait_recv())


def hand_over(*refs):
    sem = refs[8]
    copies = [pltpu.make_async_copy(refs[3], refs[7], sem.at[6])]
    for i in range(3):
        for s in range(2):
            copies.append(pltpu.make_async_copy(refs[i].at[s], refs[4 + i].at[s], sem.at[2 * i + s]))
    for copy in copies:
        copy.start()
    for copy in copies:
        copy.wait()


def shards(queries, key_rows, value_rows, out_grad, level_slope):
    seqs = queries.shape[0]
    whole = jax.ShapeDtypeStruct(queries.shape, BF16)
    any_spec = pl.BlockSpec(memory_space=pltpu.HBM)
    dma = pltpu.SemaphoreType.DMA
    held = pltpu.with_memory_space_constraint
    vmem = pltpu.VMEM
    query_grad, key_grad, value_grad, slopes = pl.pallas_call(
        kernel,
        out_shape=(whole, whole, whole, jax.ShapeDtypeStruct((2 * N,), F32)),
        in_specs=[any_spec] * 5,
        out_specs=(any_spec, any_spec, any_spec, pl.BlockSpec(memory_space=pltpu.SMEM)),
        scratch_shapes=[
            vmem((4, seqs, N, BLOCK, WIDE), BF16),
            vmem((2, seqs, 4, BLOCK, WIDE), BF16),
            vmem((2, seqs, 2, BLOCK, WIDE), BF16),
            vmem((2, seqs, 64, WIDE), BF16),
            vmem((2, seqs, 32, WIDE), BF16),
            vmem((2, seqs, 16, WIDE), BF16),
            vmem((2, seqs, UPPER, WIDE), BF16),
            vmem((N * BLOCK, LOCAL), BF16),
            vmem((N * BLOCK, UPPER), BF16),
            vmem((2, seqs, 4, PAIR, WIDE), F32),
            vmem((2, seqs, 2, BLOCK, WIDE), F32),
            vmem((2, seqs, UPPER, WIDE), F32),
            vmem((2, seqs, LOCAL, WIDE), BF16),
            vmem((2, seqs, UPPER, WIDE), BF16),
            vmem((2, seqs, UPPER, WIDE), BF16),
            vmem((3, seqs, N, BLOCK, WIDE), BF16),
            vmem((2, 8, HEAD), F32),
            vmem((N, 2, 8, HEAD), F32),
            vmem((2, 8, HEAD), F32),
            vmem((N, 2, 8, HEAD), F32),
            vmem((2, 8, HEAD), F32),
            vmem((N, 2, 8, HEAD), F32),
            pltpu.SMEM((2 * N,), F32),
            dma((1,)),
            dma((4,)),
            dma((4, N)),
            dma((4, N)),
            dma((7,)),
            dma((7,)),
            dma((7,)),
            dma((7,)),
            dma((3,)),
            dma((3, N)),
            dma((3, N)),
            dma((3, N)),
            dma((3, N)),
        ],
        compiler_params=pltpu.CompilerParams(
            collective_id=0, has_side_effects=True, vmem_limit_bytes=48 * 1024 * 1024
        ),
        name="hierarchical_attention",
    )(*(held(a, pltpu.HBM) for a in (level_slope, key_rows, value_rows, queries, out_grad)))
    return pl.pallas_call(
        hand_over,
        out_shape=(whole, whole, whole, jax.ShapeDtypeStruct((2 * N,), F32)),
        in_specs=[pl.BlockSpec(memory_space=pl.ANY)] * 4,
        out_specs=(any_spec,) * 4,
        scratch_shapes=[dma((7,))],
        compiler_params=pltpu.CompilerParams(vmem_limit_bytes=1024 * 1024),
        name="hand_over",
    )(query_grad, key_grad, value_grad, slopes)


def solution(mesh):
    placed = (P("dp", "ctx", None),) * 4 + (P(),)
    return jax.shard_map(
        shards,
        mesh=mesh,
        in_specs=placed,
        out_specs=(P("dp", "ctx", None),) * 3 + (P(),),
        check_vma=False,
    )
```
